128 devices in a mesh: lab: 4 (over y_hi, core), qry: 32 (over z, y_lo, x).
Axes of the slice: x: 4, y: 4 (y_hi: 2, y_lo: 2; y = y_hi * 2 + y_lo), z: 4, core: 2. Of those that a mesh axis runs over, the one named last changes fastest.
Arguments:
- query_hidden: bfloat16 [1024, 3584], P('qry'), may hold values from -6 to 6
- query_proj: bfloat16 [3584, 3584], P('qry', 'lab'), may hold values from -0.09375 to 0.09375
- label_hidden: bfloat16 [32768, 1536], P('qry'), may hold values from -6 to 6
- label_proj: bfloat16 [1536, 3584], P('qry', 'lab'), may hold values from -0.15625 to 0.15625
- pos_ids: int32 [1024, 8], P('qry'), may hold values from 0 to 32767
- pos_count: int32 [1024], P('qry'), may hold values from 1 to 8
Outputs:
- grad_query_proj: float32 [3584, 3584], P('qry', 'lab')
- grad_label_proj: float32 [1536, 3584], P('qry', 'lab')
- label_loss: float32 [32768], P('qry')
- grad_query_embed: float32 [1024, 3584], P('qry', 'lab')
The draws below stay inside these ranges and needn't reach their ends.
Inputs may be any that keep to these rules, and one draw needn't show every extreme that they name: `pos_ids`: label numbers of the block; only the first pos_count entries of a row are positives, the rest is padding.
All inputs are finite; a program needn't handle non-finite values.
Results may differ from the reference program's by a relative error of at most 0.004.
Values may be sent and summed in bfloat16 or wider, within the bound.
A program may use at most 128 MiB of HBM per device.

```python
import math
import jax
import jax.numpy as jnp
import numpy as np
from jax import lax

E = 3584
DL = 1536
POS = 8
Q = 1024
L = 32768


def set_ends(array, own_key, least, top_value):
    shape = array.shape
    index_at = [jax.random.randint(jax.random.fold_in(own_key, axis), (), 0, shape[axis]) for axis in range(len(shape))]
    array = array.at[tuple(index_at)].set(least)
    longest = shape.index(max(shape))
    index_at[longest] = (index_at[longest] + 1) % shape[longest]
    return array.at[tuple(index_at)].set(top_value)


def shard_levels(stream_key, extent, shards, low, largest):
    factor_of, own = 1.0, jax.random.fold_in(stream_key, 6)
    for axis_at, shards_of in shards:
        draws = jnp.exp(jax.random.uniform(jax.random.fold_in(own, axis_at), (shards_of,), jnp.float32, low / len(shards), largest / len(shards)))
        factor_of = factor_of * jnp.repeat(draws, extent[axis_at] // shards_of).reshape([-1 if axis == axis_at else 1 for axis in range(len(extent))])
    return factor_of


def rank_table(amount, lean):
    loads = [(1 << 20) // math.isqrt(grade ** lean) + 1 for grade in range(1, amount + 1)]
    scale = 1 + sum(loads) // (1 << 30)
    return np.cumsum(np.array([max(1, weight // scale) for weight in loads]))


def ranked_ids(own_key, dims, number_of, skew):
    grid = rank_table(number_of, skew)
    ticket = jax.random.randint(jax.random.fold_in(own_key, 1), dims, 0, int(grid[number_of - 1]))
    rank = jnp.searchsorted(jnp.asarray(grid, jnp.int32), ticket, side="right")
    return jax.random.permutation(jax.random.fold_in(own_key, 2), number_of)[rank].astype(jnp.int32)


def bell_draw(stream_key, dims, spread, most, cuts=(), kind=jnp.bfloat16):
    drawn = spread * jax.random.normal(stream_key, dims, jnp.float32)
    if cuts:
        drawn = drawn * shard_levels(stream_key, dims, cuts, -0.22, 0.18)
    return jnp.clip(drawn, -most, most).astype(kind)


def setup_inputs(seed: int = 0) -> dict:
    key_of = jax.random.split(jax.random.key(seed), 7)
    return {
        "query_hidden": bell_draw(key_of[0], (Q, E), 1.0, 6.0, ((0, 32),)),
        "query_proj": bell_draw(key_of[1], (E, E), E ** -0.5, 0.09375, ((0, 32), (1, 4))),
        "label_hidden": bell_draw(key_of[2], (L, DL), 1.0, 6.0, ((0, 32),)),
        "label_proj": bell_draw(key_of[3], (DL, E), DL ** -0.5, 0.15625, ((0, 32), (1, 4))),
        "pos_ids": set_ends(ranked_ids(key_of[4], (Q, POS), L, 2), jax.random.fold_in(key_of[4], 3), 0, L - 1).astype(jnp.int32),
        "pos_count": set_ends(jax.random.randint(key_of[5], (Q,), 1, POS + 1), jax.random.fold_in(key_of[5], 1), 1, POS).astype(jnp.int32),
    }


def focal_parts(logits, target, counts, temper):
    weight = (1.0 - 0.99) / (1.0 - jnp.power(jnp.float32(0.99), counts + 1.0))
    chance = jax.nn.sigmoid(logits)
    log_pos = -jax.nn.softplus(-logits)
    log_neg = -jax.nn.softplus(logits)
    rest = 1.0 - chance
    loss_terms = -(target * rest * rest * log_pos + (1.0 - target) * chance * chance * log_neg)
    slope = target * (2.0 * chance * rest * rest * log_pos - rest * rest * rest) + (1.0 - target) * (chance * chance * chance - 2.0 * chance * chance * rest * log_neg)
    return weight * loss_terms, (weight * slope * temper).astype(jnp.bfloat16)


def reference(query_hidden, query_proj, label_hidden, label_proj, pos_ids, pos_count):
    width = query_hidden.shape[1]
    temper = width ** -0.5
    n_query = query_hidden.shape[0]
    n_label = label_hidden.shape[0]
    query_embed = jnp.dot(query_hidden, query_proj, preferred_element_type=jnp.float32).astype(jnp.bfloat16)
    label_embed = jnp.dot(label_hidden, label_proj, preferred_element_type=jnp.float32).astype(jnp.bfloat16)
    logits = lax.dot_general(query_embed, label_embed, (((1,), (1,)), ((), ())), preferred_element_type=jnp.float32) * temper
    slot_ids = jnp.arange(pos_ids.shape[1], dtype=jnp.int32)
    in_use = (slot_ids[None, :] < pos_count[:, None]).astype(jnp.float32)
    row_ids = jnp.broadcast_to(jnp.arange(n_query, dtype=jnp.int32)[:, None], pos_ids.shape)
    target = jnp.zeros((n_query, n_label), jnp.float32).at[row_ids, pos_ids].max(in_use)
    counts = jax.ops.segment_sum(in_use.reshape(-1), pos_ids.reshape(-1), num_segments=n_label)
    loss_terms, grad_logits = focal_parts(logits, target, counts[None, :], temper)
    label_loss = jnp.sum(loss_terms, axis=0) / n_query
    grad_label_embed = lax.dot_general(grad_logits, query_embed, (((0,), (0,)), ((), ())), preferred_element_type=jnp.float32).astype(jnp.bfloat16)
    grad_query_embed = jnp.dot(grad_logits, label_embed, preferred_element_type=jnp.float32)
    query_embed_grad = grad_query_embed.astype(jnp.bfloat16)
    grad_label_proj = lax.dot_general(label_hidden, grad_label_embed, (((0,), (0,)), ((), ())), preferred_element_type=jnp.float32)
    grad_query_proj = lax.dot_general(query_hidden, query_embed_grad, (((0,), (0,)), ((), ())), preferred_element_type=jnp.float32)
    return grad_query_proj, grad_label_proj, label_loss, grad_query_embed
```

```python
import jax
import jax.numpy as jnp
import numpy as np
from jax import lax
from jax.experimental import pallas as pl
from jax.experimental.pallas import tpu as pltpu
from jax.sharding import PartitionSpec as P

NX, NB, NZ, NLAB, NQRY = 4, 8, 4, 4, 32
ROWS = (((0,), (0,)), ((), ()))
COLS = (((1,), (1,)), ((), ()))
MESH = pl.DeviceIdType.MESH
F32, BF16 = jnp.float32, jnp.bfloat16


def push(src, dst, send, recv, **device):
    return pltpu.make_async_remote_copy(
        src_ref=src, dst_ref=dst, send_sem=send, recv_sem=recv, device_id=device, device_id_type=MESH
    )


def dot(left, right, dims=(((1,), (0,)), ((), ()))):
    return lax.dot_general(left, right, dims, preferred_element_type=F32)


def each(count, step):
    def body(d, carry):
        step(d)
        return carry

    lax.fori_loop(1, count, body, 0)


def step_kernel(temper, n_query, qh, qp, lh, lp, ids, gqp_out, glp_out, loss_out, gqe_out, s):
    own = qh.shape[0]
    e_blk, d_blk = qh.shape[1] // NB, lh.shape[1] // NB
    e_row, d_row, width = qp.shape[0], lp.shape[0], qp.shape[1]
    n_label = lh.shape[0]
    quart = NB * own // NLAB
    here = NB * own
    d_pair = 2 * d_blk
    me, j = lax.axis_index("qry"), lax.axis_index("lab")
    x, b, z = lax.rem(me, NX), lax.div(me, NX), lax.div(me, 2 * NX)
    y = lax.rem(b, 2)
    y_peer = (2 * z + 1 - y) * NX + x

    def at_b(d):
        nb = lax.rem(b + d, NB)
        return nb, nb * NX + x

    def at_x(d):
        nx = lax.rem(x + d, NX)
        return nx, b * NX + nx

    def at_plane(d):
        nx, nz = lax.rem(x + lax.rem(d, NX), NX), lax.rem(z + lax.div(d, NX), NZ)
        return nx, nz, (2 * nz + y) * NX + nx

    def at_lab(d):
        return lax.rem(j + d, NLAB)

    def rows(index, size):
        return pl.ds(pl.multiple_of(index * size, size), size)

    fetch = pltpu.make_async_copy(lh, s.lh, s.fetch)
    fetch.start()
    for k in range(NB):
        s.q_send[k] = qh[:, k * e_blk : (k + 1) * e_blk]

    barrier = pltpu.get_barrier_semaphore()
    each(NQRY, lambda d: pl.semaphore_signal(barrier, inc=1, device_id={"qry": lax.rem(me + d, NQRY)}, device_id_type=MESH))
    each(NLAB, lambda d: pl.semaphore_signal(barrier, inc=1, device_id={"lab": at_lab(d)}, device_id_type=MESH))
    pl.semaphore_wait(barrier, NQRY - 1 + NLAB - 1)

    def hidden(d):
        nb, dev = at_b(d)
        return push(s.q_send.at[nb], s.q_blk.at[b], s.ss_a.at[d], s.rs_a.at[d], qry=dev)

    def q_rows(d):
        return push(qp, s.qp.at[rows(x, e_row)], s.ss_w.at[d], s.rs_w.at[d], qry=at_x(d)[1])

    def l_rows(d):
        return push(lp, s.lp.at[rows(x, d_row)], s.ss_d.at[d], s.rs_d.at[d], qry=at_x(d)[1])

    mine = 2 * x + y

    def positives(d):
        return push(ids, s.ids.at[mine], s.ss_i.at[d], s.rs_i.at[mine], qry=lax.rem(me + d, NQRY))

    each(NB, lambda d: hidden(d).start())
    each(NX, lambda d: q_rows(d).start())

    @pl.when(z == j)
    def _():
        each(NQRY, lambda d: positives(d).start())
        s.ids[mine] = ids[...]

    each(NX, lambda d: l_rows(d).start())
    s.q_blk[b] = s.q_send[b]
    s.qp[rows(x, e_row), :] = qp[...]
    s.lp[rows(x, d_row), :] = lp[...]

    each(NB, lambda d: hidden(d).wait_recv())
    each(NX, lambda d: q_rows(d).wait_recv())
    q_blk = s.q_blk[...].reshape(here, e_blk)
    s.q_part[...] = dot(q_blk, s.qp[...]).reshape(NB, own, width)

    def q_sum(d):
        nb, dev = at_b(d)
        return push(s.q_part.at[nb], s.q_recv.at[b], s.ss_b.at[d], s.rs_b.at[d], qry=dev)

    each(NB, lambda d: q_sum(d).start())
    s.q_recv[b] = s.q_part[b]

    def id_wait(k):
        push(ids, s.ids.at[k], s.ss_i.at[0], s.rs_i.at[k], qry=y_peer).wait_recv()

    for k in range(NB):

        @pl.when(jnp.logical_or(z != j, mine != k))
        def _():
            id_wait(k)

    local = s.ids[...].reshape(here, ids.shape[1]) - n_label * me
    wide = 256
    for c in range(n_label // wide):
        column = lax.broadcasted_iota(jnp.int32, (here, wide), 1) + c * wide
        found = jnp.zeros((here, wide), F32)
        for slot in range(ids.shape[1]):
            found += jnp.where(local[:, slot : slot + 1] == column, 1.0, 0.0)
        s.mask[:, c * wide : (c + 1) * wide] = found
        s.c_part[:, c * wide : (c + 1) * wide] = jnp.sum(found.reshape(here // 8, 8, wide), axis=0)

    def count(d):
        return push(s.c_part, s.c_recv.at[j], s.ss_c.at[d], s.rs_c.at[d], lab=at_lab(d))

    each(NLAB, lambda d: count(d).start())
    s.c_recv[j] = s.c_part[...]

    each(NB, lambda d: q_sum(d).wait_recv())
    total = s.q_recv[0]
    for k in range(1, NB):
        total += s.q_recv[k]
    s.qe[b] = total.astype(BF16)

    def q_all(d):
        return push(s.qe.at[b], s.qe.at[b], s.ss_e.at[d], s.rs_e.at[d], qry=at_b(d)[1])

    each(NB, lambda d: q_all(d).start())
    each(NX, lambda d: l_rows(d).wait_recv())
    each(NB, lambda d: q_all(d).wait_recv())

    qe = s.qe[...].reshape(here, width)
    s.t_part[...] = dot(qe, s.lp[...], COLS).reshape(NLAB, quart, d_blk)

    def t_sum(d):
        nj = at_lab(d)
        return push(s.t_part.at[nj], s.t_recv.at[j], s.ss_t.at[d], s.rs_t.at[d], lab=nj)

    each(NLAB, lambda d: t_sum(d).start())
    s.t_recv[j] = s.t_part[j]

    each(NLAB, lambda d: count(d).wait_recv())
    counts = jnp.sum(s.c_recv[0] + s.c_recv[1] + s.c_recv[2] + s.c_recv[3], axis=0, keepdims=True)
    s.weight[...] = (1.0 - 0.99) / (1.0 - jnp.exp((counts + 1.0) * float(np.log(np.float64(np.float32(0.99))))))

    each(NLAB, lambda d: t_sum(d).wait_recv())
    s.t_own[...] = (s.t_recv[0] + s.t_recv[1] + s.t_recv[2] + s.t_recv[3]).astype(BF16)
    t_swap = push(s.t_own, s.t_peer, s.ss_ty, s.rs_ty, qry=y_peer)
    t_swap.start()
    t_swap.wait_recv()

    @pl.when(y == 0)
    def _():
        s.t_pair[:, :d_blk] = s.t_own[...]
        s.t_pair[:, d_blk:] = s.t_peer[...]

    @pl.when(y == 1)
    def _():
        s.t_pair[:, :d_blk] = s.t_peer[...]
        s.t_pair[:, d_blk:] = s.t_own[...]

    def t_all(d):
        return push(
            s.t_pair, s.t.at[rows(x, quart), rows(z, d_pair)], s.ss_p.at[d], s.rs_p.at[d], qry=at_plane(d)[2]
        )

    each(NX * NZ, lambda d: t_all(d).start())
    s.t[rows(x, quart), rows(z, d_pair)] = s.t_pair[...]
    fetch.wait()
    each(NX * NZ, lambda d: t_all(d).wait_recv())

    tall = 32

    def label_block(c, carry):
        cols = rows(c, wide)
        s.logit[...] = dot(s.t[...], s.lh[cols, :], COLS) * temper
        weight = s.weight[:, cols]

        def row_block(r, loss):
            at = rows(r, tall)
            value = s.logit[at, :]
            hit = s.mask[at, cols] > 0.0
            value = jnp.where(hit, -value, value)
            small = jnp.exp(-jnp.abs(value))
            soft = jnp.maximum(value, 0.0) + jnp.log1p(small)
            over = 1.0 / (1.0 + small)
            under = small * over
            high = value >= 0.0
            chance, rest = jnp.where(high, over, under), jnp.where(high, under, over)
            square = chance * chance
            slope = weight * (square * (chance + 2.0 * rest * soft)) * temper
            s.gl[at, cols] = jnp.where(hit, -slope, slope).astype(BF16)
            return loss + jnp.sum((weight * (square * soft)).reshape(tall // 8, 8, wide), axis=0)

        s.l_part[:, cols] = lax.fori_loop(0, here // tall, row_block, jnp.zeros((8, wide), F32))
        return carry

    lax.fori_loop(0, n_label // wide, label_block, 0)

    spot = NX * z + x

    def u_sum(d):
        nx, nz, dev = at_plane(d)
        return push(s.u_part.at[rows(nx, quart), rows(nz, d_pair)], s.u_recv.at[spot], s.ss_u.at[d], s.rs_u.at[d], qry=dev)

    def u_block(k, carry):
        dz = lax.rem(k + 1, NZ)
        cols = rows(lax.rem(z + dz, NZ), d_pair)
        s.u_part[:, cols] = dot(s.gl[...], s.lh[:, cols]).astype(BF16)

        def send(dx, inner):
            @pl.when(dz * NX + dx > 0)
            def _():
                u_sum(dz * NX + dx).start()

            return inner

        lax.fori_loop(0, NX, send, 0)
        return carry

    lax.fori_loop(0, NZ, u_block, 0)

    def loss_sum(d):
        return push(s.l_part, s.l_recv.at[j], s.ss_l.at[d], s.rs_l.at[d], lab=at_lab(d))

    each(NLAB, lambda d: loss_sum(d).start())
    s.l_recv[j] = s.l_part[...]
    s.u_recv[spot] = s.u_part[rows(x, quart), rows(z, d_pair)]
    each(NX * NZ, lambda d: u_sum(d).wait_recv())
    back = s.u_recv[0].astype(F32)
    for k in range(1, NX * NZ):
        back += s.u_recv[k].astype(F32)

    @pl.when(y == 0)
    def _():
        s.u_keep[...] = back[:, :d_blk]
        s.u_give[...] = back[:, d_blk:]

    @pl.when(y == 1)
    def _():
        s.u_keep[...] = back[:, d_blk:]
        s.u_give[...] = back[:, :d_blk]

    u_swap = push(s.u_give, s.u_peer, s.ss_uy, s.rs_uy, qry=y_peer)
    u_swap.start()
    u_swap.wait_recv()
    s.u[j] = (s.u_keep[...] + s.u_peer[...]).astype(BF16)

    def u_all(d):
        return push(s.u.at[j], s.u.at[j], s.ss_v.at[d], s.rs_v.at[d], lab=at_lab(d))

    each(NLAB, lambda d: u_all(d).start())
    each(NLAB, lambda d: u_all(d).wait_recv())
    u = s.u[...].reshape(here, d_blk)

    part = dot(u, s.lp[...]).reshape(NB, own, width)
    s.g_part[...] = part
    s.g_send[...] = part.astype(BF16)

    def g_sum(d):
        nb, dev = at_b(d)
        return push(s.g_send.at[nb], s.g_recv.at[b], s.ss_g.at[d], s.rs_g.at[d], qry=dev)

    each(NB, lambda d: g_sum(d).start())
    part = dot(u, qe, ROWS).reshape(NX, d_row, width)
    s.k_part[...] = part
    s.k_send[...] = part.astype(BF16)

    def k_sum(d):
        nx, dev = at_x(d)
        return push(s.k_send.at[nx], s.k_recv.at[x], s.ss_k.at[d], s.rs_k.at[d], qry=dev)

    each(NX, lambda d: k_sum(d).start())
    each(NB, lambda d: g_sum(d).wait_recv())
    total = s.g_part[b]
    for d in range(1, NB):
        total += s.g_recv[lax.rem(b + d, NB)].astype(F32)
    gqe_out[...] = total
    s.ge[b] = total.astype(BF16)

    def g_all(d):
        return push(s.ge.at[b], s.ge.at[b], s.ss_h.at[d], s.rs_h.at[d], qry=at_b(d)[1])

    each(NB, lambda d: g_all(d).start())
    each(NLAB, lambda d: loss_sum(d).wait_recv())
    losses = jnp.sum(s.l_recv[0] + s.l_recv[1] + s.l_recv[2] + s.l_recv[3], axis=0, keepdims=True)
    loss_out[...] = losses / n_query
    each(NX, lambda d: k_sum(d).wait_recv())
    total = s.k_part[x]
    for d in range(1, NX):
        total += s.k_recv[lax.rem(x + d, NX)].astype(F32)
    glp_out[...] = total

    each(NB, lambda d: g_all(d).wait_recv())
    part = dot(s.q_blk[...].reshape(here, e_blk), s.ge[...].reshape(here, width), ROWS).reshape(NX, e_row, width)
    s.p_part[...] = part
    s.p_send[...] = part.astype(BF16)

    def p_sum(d):
        nx, dev = at_x(d)
        return push(s.p_send.at[nx], s.p_recv.at[x], s.ss_q.at[d], s.rs_q.at[d], qry=dev)

    each(NX, lambda d: p_sum(d).start())
    each(NX, lambda d: p_sum(d).wait_recv())
    total = s.p_part[x]
    for d in range(1, NX):
        total += s.p_recv[lax.rem(x + d, NX)].astype(F32)
    gqp_out[...] = total

    for copies in (hidden, q_sum, q_all, g_sum, g_all):
        each(NB, lambda d: copies(d).wait_send())
    for copies in (q_rows, l_rows, k_sum, p_sum):
        each(NX, lambda d: copies(d).wait_send())
    for copies in (count, t_sum, u_all, loss_sum):
        each(NLAB, lambda d: copies(d).wait_send())
    for copies in (t_all, u_sum):
        each(NX * NZ, lambda d: copies(d).wait_send())
    t_swap.wait_send()
    u_swap.wait_send()

    @pl.when(z == j)
    def _():
        each(NQRY, lambda d: positives(d).wait_send())


class Scratch:
    def __init__(self, names, refs):
        for name, ref in zip(names, refs):
            setattr(self, name, ref)


def shards(query_hidden, query_proj, label_hidden, label_proj, pos_ids, pos_count):
    own, wide_e = query_hidden.shape
    n_label, wide_d = label_hidden.shape
    e_row, width = query_proj.shape
    d_row = label_proj.shape[0]
    slots = pos_ids.shape[1]
    e_blk, d_blk = wide_e // NB, wide_d // NB
    here, quart = NB * own, NB * own // NLAB
    used = jnp.arange(slots, dtype=jnp.int32)[None, :] < pos_count[:, None]
    ids = jnp.where(used, pos_ids, -1)
    vmem, dma = pltpu.VMEM, pltpu.SemaphoreType.DMA
    scratch = {
        "lh": vmem((n_label, wide_d), BF16),
        "q_send": vmem((NB, own, e_blk), BF16),
        "q_blk": vmem((NB, own, e_blk), BF16),
        "qp": vmem((NX * e_row, width), BF16),
        "lp": vmem((NX * d_row, width), BF16),
        "ids": vmem((NB, own, slots), jnp.int32),
        "mask": vmem((here, n_label), F32),
        "c_part": vmem((8, n_label), F32),
        "c_recv": vmem((NLAB, 8, n_label), F32),
        "weight": vmem((1, n_label), F32),
        "q_part": vmem((NB, own, width), F32),
        "q_recv": vmem((NB, own, width), F32),
        "qe": vmem((NB, own, width), BF16),
        "t_part": vmem((NLAB, quart, d_blk), F32),
        "t_recv": vmem((NLAB, quart, d_blk), F32),
        "t_own": vmem((quart, d_blk), BF16),
        "t_peer": vmem((quart, d_blk), BF16),
        "t_pair": vmem((quart, 2 * d_blk), BF16),
        "t": vmem((here, wide_d), BF16),
        "logit": vmem((here, 256), F32),
        "gl": vmem((here, n_label), BF16),
        "l_part": vmem((8, n_label), F32),
        "l_recv": vmem((NLAB, 8, n_label), F32),
        "u_part": vmem((here, wide_d), BF16),
        "u_recv": vmem((NX * NZ, quart, 2 * d_blk), BF16),
        "u_keep": vmem((quart, d_blk), F32),
        "u_give": vmem((quart, d_blk), F32),
        "u_peer": vmem((quart, d_blk), F32),
        "u": vmem((NLAB, quart, d_blk), BF16),
        "g_part": vmem((NB, own, width), F32),
        "g_send": vmem((NB, own, width), BF16),
        "g_recv": vmem((NB, own, width), BF16),
        "ge": vmem((NB, own, width), BF16),
        "k_part": vmem((NX, d_row, width), F32),
        "k_send": vmem((NX, d_row, width), BF16),
        "k_recv": vmem((NX, d_row, width), BF16),
        "p_part": vmem((NX, e_row, width), F32),
        "p_send": vmem((NX, e_row, width), BF16),
        "p_recv": vmem((NX, e_row, width), BF16),
        "fetch": dma(()),
    }
    for name, count in (
        ("a", NB), ("w", NX), ("d", NX), ("b", NB), ("e", NB), ("c", NLAB), ("t", NLAB), ("p", NX * NZ), ("u", NX * NZ),
        ("v", NLAB), ("l", NLAB), ("g", NB), ("h", NB), ("k", NX), ("q", NX),
    ):
        scratch["ss_" + name] = dma((count,))
        scratch["rs_" + name] = dma((count,))
    scratch["ss_i"], scratch["rs_i"] = dma((NQRY,)), dma((NB,))
    for name in ("ss_ty", "rs_ty", "ss_uy", "rs_uy"):
        scratch[name] = dma(())
    names = tuple(scratch)
    in_vmem = pl.BlockSpec(memory_space=pltpu.VMEM)

    def kernel(*refs):
        step_kernel(wide_e ** (-0.5), NQRY * own, *refs[:9], Scratch(names, refs[9:]))

    gqp, glp, loss, gqe = pl.pallas_call(
        kernel,
        out_shape=(
            jax.ShapeDtypeStruct((e_row, width), F32),
            jax.ShapeDtypeStruct((d_row, width), F32),
            jax.ShapeDtypeStruct((1, n_label), F32),
            jax.ShapeDtypeStruct((own, width), F32),
        ),
        in_specs=[in_vmem, in_vmem, pl.BlockSpec(memory_space=pl.ANY), in_vmem, in_vmem],
        out_specs=(in_vmem,) * 4,
        scratch_shapes=list(scratch.values()),
        compiler_params=pltpu.CompilerParams(
            collective_id=0, has_side_effects=True, vmem_limit_bytes=48 << 20
        ),
        name="focal_step",
    )(query_hidden, query_proj, label_hidden, label_proj, ids)
    return gqp, glp, loss.reshape(n_label), gqe


def solution(mesh):
    in_specs = (
        P("qry", None),
        P("qry", "lab"),
        P("qry", None),
        P("qry", "lab"),
        P("qry", None),
        P("qry"),
    )
    out_specs = (P("qry", "lab"), P("qry", "lab"), P("qry"), P("qry", "lab"))
    return jax.shard_map(shards, mesh=mesh, in_specs=in_specs, out_specs=out_specs, check_vma=False)
```

```python
import jax
import jax.numpy as jnp
import numpy as np
from jax import lax
from jax.experimental import pallas as pl
from jax.experimental.pallas import tpu as pltpu
from jax.sharding import PartitionSpec as P

NX, NB, NZ, NLAB, NQRY = 4, 8, 4, 4, 32
ROWS = (((0,), (0,)), ((), ()))
COLS = (((1,), (1,)), ((), ()))
MESH = pl.DeviceIdType.MESH
F32, BF16 = jnp.float32, jnp.bfloat16


def push(src, dst, send, recv, **device):
    return pltpu.make_async_remote_copy(
        src_ref=src, dst_ref=dst, send_sem=send, recv_sem=recv, device_id=device, device_id_type=MESH
    )


def dot(left, right, dims=(((1,), (0,)), ((), ()))):
    return lax.dot_general(left, right, dims, preferred_element_type=F32)


def each(count, step):
    def body(d, carry):
        step(d)
        return carry

    lax.fori_loop(1, count, body, 0)


def step_kernel(temper, n_query, qh, qp, lh, lp, ids, used, gqp_out, glp_out, loss_out, gqe_out, s):
    own = qh.shape[0]
    e_blk, d_blk = qh.shape[1] // NB, lh.shape[1] // NB
    e_row, d_row, width = qp.shape[0], lp.shape[0], qp.shape[1]
    n_label = lh.shape[0]
    quart = NB * own // NLAB
    here = NB * own
    d_pair = 2 * d_blk
    me, j = lax.axis_index("qry"), lax.axis_index("lab")
    x, b, z = lax.rem(me, NX), lax.div(me, NX), lax.div(me, 2 * NX)
    y = lax.rem(b, 2)
    y_peer = (2 * z + 1 - y) * NX + x

    def at_b(d):
        nb = lax.rem(b + d, NB)
        return nb, nb * NX + x

    def at_x(d):
        nx = lax.rem(x + d, NX)
        return nx, b * NX + nx

    def at_z(d):
        nz = lax.rem(z + d, NZ)
        return nz, (2 * nz + y) * NX + x

    def at_plane(d):
        nx, nz = lax.rem(x + lax.rem(d, NX), NX), lax.rem(z + lax.div(d, NX), NZ)
        return nx, nz, (2 * nz + y) * NX + nx

    def at_lab(d):
        return lax.rem(j + d, NLAB)

    def rows(index, size):
        return pl.ds(pl.multiple_of(index * size, size), size)

    sent = []

    def start(count, copies):
        each(count, lambda d: copies(d).start())
        sent.append((count, copies))

    def arrive(count, copies):
        each(count, lambda d: copies(d).wait_recv())

    loads = [
        pltpu.make_async_copy(source, target, s.load.at[k])
        for k, (source, target) in enumerate(
            (
                (qh, s.qh),
                (ids, s.ids_raw),
                (used, s.used),
                (qp, s.qp.at[rows(x, e_row)]),
                (lp, s.lp.at[rows(x, d_row)]),
                (lh, s.lh),
            )
        )
    ]
    for load in loads:
        load.start()

    barrier = pltpu.get_barrier_semaphore()
    each(NX * NZ, lambda d: pl.semaphore_signal(barrier, inc=1, device_id={"qry": at_plane(d)[2]}, device_id_type=MESH))
    for d in range(1, NB, 2):
        pl.semaphore_signal(barrier, inc=1, device_id={"qry": at_b(d)[1]}, device_id_type=MESH)
    each(NLAB, lambda d: pl.semaphore_signal(barrier, inc=1, device_id={"lab": at_lab(d)}, device_id_type=MESH))
    loads[0].wait()
    for k in range(NB):
        s.q_send[k] = s.qh[:, k * e_blk : (k + 1) * e_blk]
    loads[1].wait()
    loads[2].wait()
    slots = ids.shape[0]
    s.ids_send[...] = jnp.full(s.ids_send.shape, -1, jnp.int32)
    slot_at = lax.broadcasted_iota(jnp.int32, ids.shape, 0)
    s.ids_send[:, :own] = jnp.where(slot_at < s.used[...], s.ids_raw[...], -1)
    pl.semaphore_wait(barrier, NX * NZ - 1 + NB // 2 + NLAB - 1)

    def hidden(d):
        nb, dev = at_b(d)
        return push(s.q_send.at[nb], s.q_blk.at[b], s.ss_a.at[d], s.rs_a.at[d], qry=dev)

    def q_rows(d):
        return push(qp, s.qp.at[rows(x, e_row)], s.ss_w.at[d], s.rs_w.at[d], qry=at_x(d)[1])

    def l_rows(d):
        return push(lp, s.lp.at[rows(x, d_row)], s.ss_d.at[d], s.rs_d.at[d], qry=at_x(d)[1])

    mine = 2 * x + y
    ids_swap = push(s.ids_send, s.ids.at[mine], s.ss_iy, s.rs_iy, qry=y_peer)

    def positives(d):
        return push(
            s.ids.at[pl.ds(2 * x, 2)], s.ids.at[pl.ds(2 * x, 2)], s.ss_i.at[d], s.rs_i.at[x], qry=at_plane(d)[2]
        )

    start(NB, hidden)
    start(NX, q_rows)

    @pl.when(z == j)
    def _():
        ids_swap.start()
        s.ids[mine] = s.ids_send[...]
        ids_swap.wait_recv()
        each(NX * NZ, lambda d: positives(d).start())

    def ids_arrive():
        for k in range(NX):

            @pl.when(jnp.logical_or(z != j, x != k))
            def _():
                pair = s.ids.at[pl.ds(2 * k, 2)]
                push(pair, pair, s.ss_i.at[0], s.rs_i.at[k], qry=y_peer).wait_recv()

    def ids_sent():
        @pl.when(z == j)
        def _():
            ids_swap.wait_send()
            each(NX * NZ, lambda d: positives(d).wait_send())

    s.q_blk[b] = s.q_send[b]
    loads[3].wait()

    arrive(NB, hidden)
    arrive(NX, q_rows)
    start(NX, l_rows)
    q_blk = s.q_blk[...].reshape(here, e_blk)
    s.q_part[...] = dot(q_blk, s.qp[...]).reshape(NB, own, width)

    def q_sum(d):
        nb, dev = at_b(d)
        return push(s.q_part.at[nb], s.q_recv.at[b], s.ss_b.at[d], s.rs_b.at[d], qry=dev)

    start(NB, q_sum)
    s.q_recv[b] = s.q_part[b]

    ids_arrive()
    local = s.ids[...].reshape(NB * slots, s.ids.shape[2]).T - n_label * me
    wide = 256
    for c in range(n_label // wide):
        column = lax.broadcasted_iota(jnp.int32, (own, wide), 1) + c * wide
        tally = jnp.zeros((8, wide), F32)
        for k in range(NB):
            found = jnp.zeros((own, wide), F32)
            for slot in range(k * slots, (k + 1) * slots):
                found += jnp.where(local[:own, slot : slot + 1] == column, 1.0, 0.0)
            s.mask[k * own : (k + 1) * own, c * wide : (c + 1) * wide] = found
            tally += jnp.sum(found.reshape(own // 8, 8, wide), axis=0)
        s.c_part[:, c * wide : (c + 1) * wide] = tally

    def count(d):
        return push(s.c_part, s.c_recv.at[j], s.ss_c.at[d], s.rs_c.at[d], lab=at_lab(d))

    start(NLAB, count)
    s.c_recv[j] = s.c_part[...]

    arrive(NB, q_sum)
    total = s.q_recv[0]
    for k in range(1, NB):
        total += s.q_recv[k]
    s.qe[b] = total.astype(BF16)

    def q_all(d):
        return push(s.qe.at[b], s.qe.at[b], s.ss_e.at[d], s.rs_e.at[d], qry=at_b(d)[1])

    start(NB, q_all)
    loads[4].wait()
    arrive(NX, l_rows)
    arrive(NB, q_all)

    qe = s.qe[...].reshape(here, width)
    s.t_part[...] = dot(qe, s.lp[...], COLS).reshape(NLAB, quart, d_blk)

    def t_sum(d):
        nj = at_lab(d)
        return push(s.t_part.at[nj], s.t_recv.at[j], s.ss_t.at[d], s.rs_t.at[d], lab=nj)

    start(NLAB, t_sum)
    s.t_recv[j] = s.t_part[j]

    arrive(NLAB, count)
    counts = jnp.sum(s.c_recv[0] + s.c_recv[1] + s.c_recv[2] + s.c_recv[3], axis=0, keepdims=True)
    s.weight[...] = (1.0 - 0.99) / (1.0 - jnp.exp((counts + 1.0) * float(np.log(np.float64(np.float32(0.99))))))

    arrive(NLAB, t_sum)
    s.t_own[...] = (s.t_recv[0] + s.t_recv[1] + s.t_recv[2] + s.t_recv[3]).astype(BF16)
    t_swap = push(s.t_own, s.t_peer, s.ss_ty, s.rs_ty, qry=y_peer)
    t_swap.start()
    t_swap.wait_recv()

    @pl.when(y == 0)
    def _():
        s.t_pair[:, :d_blk] = s.t_own[...]
        s.t_pair[:, d_blk:] = s.t_peer[...]

    @pl.when(y == 1)
    def _():
        s.t_pair[:, :d_blk] = s.t_peer[...]
        s.t_pair[:, d_blk:] = s.t_own[...]

    s.t[x, 0, :, rows(z, d_pair)] = s.t_pair[:own, :]
    s.t[x, 1, :, rows(z, d_pair)] = s.t_pair[own:, :]

    def t_x(d):
        spot = s.t.at[x, 0, :, rows(z, d_pair)]
        return push(spot, spot, s.ss_t1.at[d], s.rs_t1.at[d], qry=at_x(d)[1])

    def t_z(d):
        spot = s.t.at[x, 1, :, rows(z, d_pair)]
        return push(spot, spot, s.ss_t2.at[d], s.rs_t2.at[d], qry=at_z(d)[1])

    def t_xz(d):
        spot = s.t.at[:, 0, :, rows(z, d_pair)]
        return push(spot, spot, s.ss_t3.at[d], s.rs_t3.at[d], qry=at_z(d)[1])

    def t_zx(d):
        spot = s.t.at[x, 1]
        return push(spot, spot, s.ss_t4.at[d], s.rs_t4.at[d], qry=at_x(d)[1])

    start(NX, t_x)
    start(NZ, t_z)
    arrive(NX, t_x)
    start(NZ, t_xz)
    arrive(NZ, t_z)
    start(NX, t_zx)
    loads[5].wait()
    arrive(NZ, t_xz)
    arrive(NX, t_zx)

    tall = 32

    def label_block(c, carry):
        cols = rows(c, wide)
        s.logit[...] = dot(s.t[...].reshape(here, NB * d_blk), s.lh[cols, :], COLS) * temper
        weight = s.weight[:, cols]

        def row_block(r, loss):
            at = rows(r, tall)
            value = s.logit[at, :]
            hit = s.mask[at, cols] > 0.0
            value = jnp.where(hit, -value, value)
            small = jnp.exp(-jnp.abs(value))
            soft = jnp.maximum(value, 0.0) + jnp.log1p(small)
            over = 1.0 / (1.0 + small)
            under = small * over
            high = value >= 0.0
            chance, rest = jnp.where(high, over, under), jnp.where(high, under, over)
            square = chance * chance
            slope = weight * (square * (chance + 2.0 * rest * soft)) * temper
            s.gl[at, cols] = jnp.where(hit, -slope, slope).astype(BF16)
            return loss + jnp.sum((weight * (square * soft)).reshape(tall // 8, 8, wide), axis=0)

        s.l_part[:, cols] = lax.fori_loop(0, here // tall, row_block, jnp.zeros((8, wide), F32))
        return carry

    lax.fori_loop(0, n_label // wide, label_block, 0)

    def u_z(d):
        nz, dev = at_z(d)
        return push(s.u_part.at[:, 0, :, rows(nz, d_pair)], s.u_rz.at[z], s.ss_u1.at[d], s.rs_u1.at[d], qry=dev)

    def u_x(d):
        nx, dev = at_x(d)
        return push(s.u_part.at[nx, 1], s.u_rx.at[x], s.ss_u2.at[d], s.rs_u2.at[d], qry=dev)

    def u_zx(d):
        nx, dev = at_x(d)
        return push(s.u_sz.at[nx], s.u_rzx.at[x], s.ss_u3.at[d], s.rs_u3.at[d], qry=dev)

    def u_xz(d):
        nz, dev = at_z(d)
        return push(s.u_sx.at[:, rows(nz, d_pair)], s.u_rxz.at[z], s.ss_u4.at[d], s.rs_u4.at[d], qry=dev)

    def u_block(d):
        cols = rows(lax.rem(z + d, NZ), d_pair)
        part = dot(s.gl[...], s.lh[:, cols])
        s.u_part[:, :, :, cols] = part.astype(BF16).reshape(NX, 2, own, d_pair)

    def u_turn(d):
        u_block(d)
        u_z(d).start()

    each(NZ, u_turn)
    sent.append((NZ, u_z))
    u_block(0)
    start(NX, u_x)
    def loss_sum(d):
        return push(s.l_part, s.l_recv.at[j], s.ss_l.at[d], s.rs_l.at[d], lab=at_lab(d))

    start(NLAB, loss_sum)
    s.l_recv[j] = s.l_part[...]
    arrive(NZ, u_z)
    half = s.u_part[:, 0, :, rows(z, d_pair)].astype(F32)
    for d in range(1, NZ):
        half += s.u_rz[lax.rem(z + d, NZ)].astype(F32)
    s.u_sz[...] = half.astype(BF16)
    start(NX, u_zx)
    arrive(NX, u_x)
    half = s.u_part[x, 1].astype(F32)
    for d in range(1, NX):
        half += s.u_rx[lax.rem(x + d, NX)].astype(F32)
    s.u_sx[...] = half.astype(BF16)
    start(NZ, u_xz)
    arrive(NX, u_zx)
    half = s.u_sz[x].astype(F32)
    for d in range(1, NX):
        half += s.u_rzx[lax.rem(x + d, NX)].astype(F32)
    s.back[:own, :] = half
    arrive(NZ, u_xz)
    half = s.u_sx[:, rows(z, d_pair)].astype(F32)
    for d in range(1, NZ):
        half += s.u_rxz[lax.rem(z + d, NZ)].astype(F32)
    s.back[own:, :] = half
    back = s.back[...]

    @pl.when(y == 0)
    def _():
        s.u_keep[...] = back[:, :d_blk]
        s.u_give[...] = back[:, d_blk:]

    @pl.when(y == 1)
    def _():
        s.u_keep[...] = back[:, d_blk:]
        s.u_give[...] = back[:, :d_blk]

    u_swap = push(s.u_give, s.u_peer, s.ss_uy, s.rs_uy, qry=y_peer)
    u_swap.start()
    u_swap.wait_recv()
    s.u[j] = (s.u_keep[...] + s.u_peer[...]).astype(BF16)

    def u_all(d):
        return push(s.u.at[j], s.u.at[j], s.ss_v.at[d], s.rs_v.at[d], lab=at_lab(d))

    start(NLAB, u_all)
    arrive(NLAB, u_all)
    u = s.u[...].reshape(here, d_blk)

    part = dot(u, s.lp[...]).reshape(NB, own, width)
    s.g_part[...] = part
    s.g_send[...] = part.astype(BF16)

    def g_sum(d):
        nb, dev = at_b(d)
        return push(s.g_send.at[nb], s.g_recv.at[b], s.ss_g.at[d], s.rs_g.at[d], qry=dev)

    start(NB, g_sum)
    part = dot(u, qe, ROWS).reshape(NX, d_row, width)
    s.k_part[...] = part
    s.k_send[...] = part.astype(BF16)

    def k_sum(d):
        nx, dev = at_x(d)
        return push(s.k_send.at[nx], s.k_recv.at[x], s.ss_k.at[d], s.rs_k.at[d], qry=dev)

    start(NX, k_sum)
    arrive(NB, g_sum)
    total = s.g_part[b]
    for d in range(1, NB):
        total += s.g_recv[lax.rem(b + d, NB)].astype(F32)
    gqe_out[...] = total
    s.ge[b] = total.astype(BF16)

    def g_all(d):
        return push(s.ge.at[b], s.ge.at[b], s.ss_h.at[d], s.rs_h.at[d], qry=at_b(d)[1])

    start(NB, g_all)
    arrive(NLAB, loss_sum)
    losses = jnp.sum(s.l_recv[0] + s.l_recv[1] + s.l_recv[2] + s.l_recv[3], axis=0, keepdims=True)
    loss_out[...] = losses / n_query
    arrive(NX, k_sum)
    total = s.k_part[x]
    for d in range(1, NX):
        total += s.k_recv[lax.rem(x + d, NX)].astype(F32)
    glp_out[...] = total

    arrive(NB, g_all)
    part = dot(s.q_blk[...].reshape(here, e_blk), s.ge[...].reshape(here, width), ROWS).reshape(NX, e_row, width)
    s.p_part[...] = part
    s.p_send[...] = part.astype(BF16)

    def p_sum(d):
        nx, dev = at_x(d)
        return push(s.p_send.at[nx], s.p_recv.at[x], s.ss_q.at[d], s.rs_q.at[d], qry=dev)

    start(NX, p_sum)
    arrive(NX, p_sum)
    total = s.p_part[x]
    for d in range(1, NX):
        total += s.p_recv[lax.rem(x + d, NX)].astype(F32)
    gqp_out[...] = total

    for number, copies in sent:
        each(number, lambda d: copies(d).wait_send())
    t_swap.wait_send()
    u_swap.wait_send()
    ids_sent()


class Scratch:
    def __init__(self, names, refs):
        for name, ref in zip(names, refs):
            setattr(self, name, ref)


def shards(query_hidden, query_proj, label_hidden, label_proj, pos_ids, pos_count):
    own, wide_e = query_hidden.shape
    n_label, wide_d = label_hidden.shape
    e_row, width = query_proj.shape
    d_row = label_proj.shape[0]
    slots = pos_ids.shape[1]
    e_blk, d_blk = wide_e // NB, wide_d // NB
    here, quart = NB * own, NB * own // NLAB
    vmem, dma = pltpu.VMEM, pltpu.SemaphoreType.DMA
    scratch = {
        "lh": vmem((n_label, wide_d), BF16),
        "q_send": vmem((NB, own, e_blk), BF16),
        "q_blk": vmem((NB, own, e_blk), BF16),
        "qp": vmem((NX * e_row, width), BF16),
        "lp": vmem((NX * d_row, width), BF16),
        "qh": vmem((own, wide_e), BF16),
        "ids_raw": vmem((slots, own), jnp.int32),
        "used": vmem((1, own), jnp.int32),
        "ids_send": vmem((slots, 128), jnp.int32),
        "ids": vmem((NB, slots, 128), jnp.int32),
        "mask": vmem((here, n_label), F32),
        "c_part": vmem((8, n_label), F32),
        "c_recv": vmem((NLAB, 8, n_label), F32),
        "weight": vmem((1, n_label), F32),
        "q_part": vmem((NB, own, width), F32),
        "q_recv": vmem((NB, own, width), F32),
        "qe": vmem((NB, own, width), BF16),
        "t_part": vmem((NLAB, quart, d_blk), F32),
        "t_recv": vmem((NLAB, quart, d_blk), F32),
        "t_own": vmem((quart, d_blk), BF16),
        "t_peer": vmem((quart, d_blk), BF16),
        "t_pair": vmem((quart, 2 * d_blk), BF16),
        "t": vmem((NX, 2, own, wide_d), BF16),
        "logit": vmem((here, 256), F32),
        "gl": vmem((here, n_label), BF16),
        "l_part": vmem((8, n_label), F32),
        "l_recv": vmem((NLAB, 8, n_label), F32),
        "u_part": vmem((NX, 2, own, wide_d), BF16),
        "u_rz": vmem((NZ, NX, own, 2 * d_blk), BF16),
        "u_rx": vmem((NX, own, wide_d), BF16),
        "u_sz": vmem((NX, own, 2 * d_blk), BF16),
        "u_sx": vmem((own, wide_d), BF16),
        "u_rzx": vmem((NX, own, 2 * d_blk), BF16),
        "u_rxz": vmem((NZ, own, 2 * d_blk), BF16),
        "back": vmem((quart, 2 * d_blk), F32),
        "u_keep": vmem((quart, d_blk), F32),
        "u_give": vmem((quart, d_blk), F32),
        "u_peer": vmem((quart, d_blk), F32),
        "u": vmem((NLAB, quart, d_blk), BF16),
        "g_part": vmem((NB, own, width), F32),
        "g_send": vmem((NB, own, width), BF16),
        "g_recv": vmem((NB, own, width), BF16),
        "ge": vmem((NB, own, width), BF16),
        "k_part": vmem((NX, d_row, width), F32),
        "k_send": vmem((NX, d_row, width), BF16),
        "k_recv": vmem((NX, d_row, width), BF16),
        "p_part": vmem((NX, e_row, width), F32),
        "p_send": vmem((NX, e_row, width), BF16),
        "p_recv": vmem((NX, e_row, width), BF16),
        "load": dma((6,)),
    }
    for name, count in (
        ("a", NB), ("w", NX), ("d", NX), ("b", NB), ("e", NB), ("c", NLAB), ("t", NLAB), ("t1", NX), ("t2", NZ), ("t3", NZ), ("t4", NX),
        ("u1", NZ), ("u2", NX), ("u3", NX), ("u4", NZ),
        ("v", NLAB), ("l", NLAB), ("g", NB), ("h", NB), ("k", NX), ("q", NX),
    ):
        scratch["ss_" + name] = dma((count,))
        scratch["rs_" + name] = dma((count,))
    scratch["ss_i"], scratch["rs_i"] = dma((NX * NZ,)), dma((NX,))
    for name in ("ss_ty", "rs_ty", "ss_uy", "rs_uy", "ss_iy", "rs_iy"):
        scratch[name] = dma(())
    names = tuple(scratch)
    in_vmem = pl.BlockSpec(memory_space=pltpu.VMEM)

    def kernel(*refs):
        step_kernel(wide_e ** (-0.5), NQRY * own, *refs[:10], Scratch(names, refs[10:]))

    arrays = [
        pltpu.with_memory_space_constraint(a, pltpu.HBM)
        for a in (query_hidden, query_proj, label_hidden, label_proj, pos_ids.T, pos_count.reshape(1, own))
    ]
    gqp, glp, loss, gqe = pl.pallas_call(
        kernel,
        out_shape=(
            jax.ShapeDtypeStruct((e_row, width), F32),
            jax.ShapeDtypeStruct((d_row, width), F32),
            jax.ShapeDtypeStruct((1, n_label), F32),
            jax.ShapeDtypeStruct((own, width), F32),
        ),
        in_specs=[pl.BlockSpec(memory_space=pltpu.HBM)] * 6,
        out_specs=(in_vmem,) * 4,
        scratch_shapes=list(scratch.values()),
        compiler_params=pltpu.CompilerParams(
            collective_id=0, has_side_effects=True, vmem_limit_bytes=48 << 20
        ),
        name="focal_step",
    )(*arrays)
    return gqp, glp, loss.reshape(n_label), gqe


def solution(mesh):
    in_specs = (
        P("qry", None),
        P("qry", "lab"),
        P("qry", None),
        P("qry", "lab"),
        P("qry", None),
        P("qry"),
    )
    out_specs = (P("qry", "lab"), P("qry", "lab"), P("qry"), P("qry", "lab"))
    return jax.shard_map(shards, mesh=mesh, in_specs=in_specs, out_specs=out_specs, check_vma=False)
```

```python
import jax
import jax.numpy as jnp
import numpy as np
from jax import lax
from jax.experimental import pallas as pl
from jax.experimental.pallas import tpu as pltpu
from jax.sharding import PartitionSpec as P

NX, NY, NZ, NLAB = 4, 2, 4, 4
NQRY = NX * NY * NZ
ROWS = (((0,), (0,)), ((), ()))
COLS = (((1,), (1,)), ((), ()))
MESH = pl.DeviceIdType.MESH
F32, BF16 = jnp.float32, jnp.bfloat16


def dot(left, right, dims=(((1,), (0,)), ((), ()))):
    return lax.dot_general(left, right, dims, preferred_element_type=F32)


def each(count, step):
    def body(d, carry):
        step(d)
        return carry

    lax.fori_loop(1, count, body, 0)


def step_kernel(temper, cut, qh, qp, lh, lp, ids, used, gqp_out, glp_out, loss_out, gqe_out, s):
    own = qh.shape[0]
    e_row, d_row, width = qp.shape[0], lp.shape[0], qp.shape[1]
    n_label, wide_d = lh.shape
    e_z, d_z = NX * NY * e_row, NX * NY * d_row
    e_b = NX * e_row
    here, block = NX * NY * own, NZ * own
    me, j = lax.axis_index("qry"), lax.axis_index("lab")
    x, y, z = lax.rem(me, NX), lax.rem(lax.div(me, NX), NY), lax.div(me, NX * NY)

    def at(nz, ny, nx):
        return {"qry": (nz * NY + ny) * NX + nx}

    y_peer = at(z, 1 - y, x)

    def next_x(d):
        return lax.rem(x + d, NX)

    def next_z(d):
        return lax.rem(z + d, NZ)

    def next_lab(d):
        return lax.rem(j + d, NLAB)

    def rows(index, size):
        return pl.ds(pl.multiple_of(index * size, size), size)

    def push(name, d, src, dst, device):
        return pltpu.make_async_remote_copy(
            src_ref=src,
            dst_ref=dst,
            send_sem=getattr(s, "send_" + name).at[d],
            recv_sem=getattr(s, "recv_" + name).at[d],
            device_id=device,
            device_id_type=MESH,
        )

    sent = []

    def start(count, copies):
        each(count, lambda d: copies(d).start())
        sent.append((count, copies))

    def arrive(count, copies):
        each(count, lambda d: copies(d).wait_recv())

    loads = [
        pltpu.make_async_copy(source, target, s.load.at[k])
        for k, (source, target) in enumerate(
            (
                (qh, s.qh),
                (ids, s.ids_raw),
                (used, s.used),
                (qp.at[:, pl.ds(0, cut)], s.wx.at[y, x]),
                (qp.at[:, pl.ds(cut, width - cut)], s.wz.at[z, y]),
                (lp, s.lp.at[y, x]),
                (lh, s.lh),
            )
        )
    ]
    for load in loads:
        load.start()

    barrier = pltpu.get_barrier_semaphore()

    def greet(device):
        pl.semaphore_signal(barrier, inc=1, device_id=device, device_id_type=MESH)

    each(NX, lambda d: greet(at(z, y, next_x(d))))
    each(NZ, lambda d: greet(at(next_z(d), y, x)))
    greet(y_peer)
    each(NX, lambda d: greet(at(z, 1 - y, next_x(d))))
    each(NZ, lambda d: greet(at(next_z(d), 1 - y, x)))
    each(NLAB, lambda d: greet({"lab": next_lab(d)}))

    loads[0].wait()
    for k in range(NX):
        s.q1_send[k] = jnp.concatenate(
            [s.qh[:, (NX * r + k) * e_row : (NX * r + k + 1) * e_row] for r in range(NZ * NY)], axis=1
        )
    for k in range(NZ * NY):
        s.qx_send[k] = s.qh[:, k * e_b : (k + 1) * e_b]
    for nx in range(NX):
        for ny in range(NY):
            first = [(NX * (NY * r + ny) + nx) * e_row for r in range(NZ)]
            s.qz_send[NY * nx + ny] = jnp.concatenate([s.qh[:, f : f + e_row] for f in first], axis=1)
    loads[1].wait()
    loads[2].wait()
    slots = ids.shape[0]
    s.ids_send[...] = jnp.full(s.ids_send.shape, -1, jnp.int32)
    slot_at = lax.broadcasted_iota(jnp.int32, ids.shape, 0)
    s.ids_send[:, :own] = jnp.where(slot_at < s.used[...], s.ids_raw[...], -1)
    pl.semaphore_wait(barrier, 2 * (NX - 1) + 2 * (NZ - 1) + 1 + NLAB - 1)

    x_cols, z_cols = pl.ds(0, cut), pl.ds(cut, width - cut)

    def w_yx(d):
        return push("w_yx", d, qp.at[:, x_cols], s.wx.at[y, x], y_peer)

    def w_yz(d):
        return push("w_yz", d, qp.at[:, z_cols], s.wz.at[z, y], y_peer)

    def w_x(d):
        return push("w_x", d, qp.at[:, x_cols], s.wx.at[y, x], at(z, y, next_x(d)))

    def w_z(d):
        return push("w_z", d, qp.at[:, z_cols], s.wz.at[z, y], at(next_z(d), y, x))

    def w_fx(d):
        return push("w_fx", d, s.wx.at[1 - y, x], s.wx.at[1 - y, x], at(z, y, next_x(d)))

    def w_fz(d):
        return push("w_fz", d, s.wz.at[z, 1 - y], s.wz.at[z, 1 - y], at(next_z(d), y, x))

    def q0(d):
        return push("q0", d, qh.at[:, rows(next_z(d), e_z)], s.q0.at[z], at(next_z(d), y, x))

    def q1(d):
        return push("q1", d, s.q1_send.at[next_x(d)], s.q1.at[x], at(z, y, next_x(d)))

    def l_x(d):
        return push("l_x", d, lp, s.lp.at[y, x], at(z, y, next_x(d)))

    def l_y(d):
        return push("l_y", d, s.lp.at[y], s.lp.at[y], y_peer)

    start(2, w_yx)
    start(2, w_yz)
    start(NX, w_x)
    start(NZ, w_z)
    start(NZ, q0)
    start(NX, q1)
    start(NX, l_x)

    def i_y(d):
        return push("i_y", d, s.ids_send, s.ids.at[x, y], y_peer)

    def i_x(d):
        return push("i_x", d, s.ids.at[x], s.ids.at[x], at(z, y, next_x(d)))

    def i_z(d):
        return push("i_z", d, s.ids, s.ids, at(next_z(d), y, x))

    holder = z == j

    @pl.when(holder)
    def _():
        i_y(1).start()
        s.ids[x, y] = s.ids_send[...]
        i_y(1).wait_recv()
        each(NX, lambda d: i_x(d).start())

    s.q0[z] = s.qh[:, rows(z, e_z)]
    s.q1[x] = s.q1_send[x]
    arrive(2, w_yx)
    start(NX, w_fx)
    arrive(2, w_yz)
    start(NZ, w_fz)

    @pl.when(holder)
    def _():
        arrive(NX, i_x)
        each(NZ, lambda d: i_z(d).start())

    def ids_arrive():
        @pl.when(jnp.logical_not(holder))
        def _():
            i_z(lax.rem(z - j + NZ, NZ)).wait_recv()

    def ids_sent():
        @pl.when(holder)
        def _():
            i_y(1).wait_send()
            each(NX, lambda d: i_x(d).wait_send())
            each(NZ, lambda d: i_z(d).wait_send())

    arrive(NX, l_x)
    loads[5].wait()
    start(2, l_y)

    arrive(NZ, q0)
    arrive(NX, w_x)
    loads[3].wait()
    arrive(NX, w_fx)
    s.part_z[...] = dot(s.q0[...].reshape(block, e_z), s.wx[...].reshape(e_z, cut)).reshape(NZ, own, cut)

    def b_z(d):
        return push("b_z", d, s.part_z.at[next_z(d)], s.sum_z.at[z], at(next_z(d), y, x))

    start(NZ, b_z)
    arrive(NX, q1)
    arrive(NZ, w_z)
    loads[4].wait()
    arrive(NZ, w_fz)
    s.part_x[...] = dot(s.q1[...].reshape(block, e_z), s.wz[...].reshape(e_z, width - cut)).reshape(NX, own, width - cut)

    def b_x(d):
        return push("b_x", d, s.part_x.at[next_x(d)], s.sum_x.at[x], at(z, y, next_x(d)))

    start(NX, b_x)
    s.sum_z[z] = s.part_z[z]
    s.sum_x[x] = s.part_x[x]

    ids_arrive()
    local = s.ids[...].reshape(NX * NY * slots, s.ids.shape[3]).T - n_label * me
    wide = 256
    for c in range(n_label // wide):
        column = lax.broadcasted_iota(jnp.int32, (own, wide), 1) + c * wide
        tally = jnp.zeros((8, wide), F32)
        for k in range(NX * NY):
            found = jnp.zeros((own, wide), F32)
            for slot in range(k * slots, (k + 1) * slots):
                found += jnp.where(local[:own, slot : slot + 1] == column, 1.0, 0.0)
            s.mask[k * own : (k + 1) * own, c * wide : (c + 1) * wide] = found
            tally += jnp.sum(found.reshape(own // 8, 8, wide), axis=0)
        s.c_part[:, c * wide : (c + 1) * wide] = tally

    def count(d):
        return push("count", d, s.c_part, s.c_recv.at[j], {"lab": next_lab(d)})

    start(NLAB, count)
    s.c_recv[j] = s.c_part[...]

    arrive(NZ, b_z)
    s.qe[z, :, :cut] = (s.sum_z[0] + s.sum_z[1] + s.sum_z[2] + s.sum_z[3]).astype(BF16)
    arrive(NX, b_x)
    s.qe[z, :, cut:] = (s.sum_x[0] + s.sum_x[1] + s.sum_x[2] + s.sum_x[3]).astype(BF16)

    def q_all(d):
        return push("q_all", d, s.qe.at[z], s.qe.at[z], at(next_z(d), y, x))

    start(NZ, q_all)
    arrive(2, l_y)
    arrive(NZ, q_all)

    s.t_part[...] = dot(s.qe[...].reshape(block, width), s.lp[...].reshape(d_z, width), COLS).reshape(NLAB, own, d_z)

    def t_sum(d):
        return push("t_sum", d, s.t_part.at[next_lab(d)], s.t_recv.at[j], {"lab": next_lab(d)})

    start(NLAB, t_sum)
    s.t_recv[j] = s.t_part[j]

    arrive(NLAB, count)
    counts = jnp.sum(s.c_recv[0] + s.c_recv[1] + s.c_recv[2] + s.c_recv[3], axis=0, keepdims=True)
    s.weight[...] = (1.0 - 0.99) / (1.0 - jnp.exp((counts + 1.0) * float(np.log(np.float64(np.float32(0.99))))))

    arrive(NLAB, t_sum)
    mine = rows(z, d_z)
    s.t[x, y, :, mine] = (s.t_recv[0] + s.t_recv[1] + s.t_recv[2] + s.t_recv[3]).astype(BF16)

    def t_y(d):
        return push("t_y", d, s.t.at[x, y, :, mine], s.t.at[x, y, :, mine], y_peer)

    def t_x(d):
        return push("t_x", d, s.t.at[x, 0, :, mine], s.t.at[x, 0, :, mine], at(z, y, next_x(d)))

    def t_z(d):
        return push("t_z", d, s.t.at[x, 1, :, mine], s.t.at[x, 1, :, mine], at(next_z(d), y, x))

    def t_xz(d):
        return push("t_xz", d, s.t.at[:, 0, :, mine], s.t.at[:, 0, :, mine], at(next_z(d), y, x))

    def t_zx(d):
        return push("t_zx", d, s.t.at[x, 1], s.t.at[x, 1], at(z, y, next_x(d)))

    start(2, t_y)
    arrive(2, t_y)
    start(NX, t_x)
    start(NZ, t_z)
    arrive(NX, t_x)
    start(NZ, t_xz)
    arrive(NZ, t_z)
    start(NX, t_zx)
    loads[6].wait()
    arrive(NZ, t_xz)
    arrive(NX, t_zx)

    def in_b(d):
        return lax.rem(z + lax.div(d, NY), NZ), lax.rem(y + lax.rem(d, NY), NY)

    def in_c(d):
        return lax.rem(x + lax.div(d, NY), NX), lax.rem(y + lax.rem(d, NY), NY)

    spot_b, spot_c = NY * z + y, NY * x + y

    def q_bx(d):
        nz, ny = in_b(d)
        return push("q_bx", d, s.qx_send.at[NY * nz + ny], s.qx.at[spot_b], at(nz, ny, x))

    def q_bz(d):
        nx, ny = in_c(d)
        return push("q_bz", d, s.qz_send.at[NY * nx + ny], s.qz.at[spot_c], at(z, ny, nx))

    start(NZ * NY, q_bx)
    start(NX * NY, q_bz)
    s.qx[spot_b] = s.qx_send[spot_b]
    s.qz[spot_c] = s.qz_send[spot_c]

    tall = 32

    def label_block(c, carry):
        cols = rows(c, wide)
        s.logit[...] = dot(s.t[...].reshape(here, wide_d), s.lh[cols, :], COLS) * temper
        weight = s.weight[:, cols]

        def row_block(r, loss):
            some = rows(r, tall)
            value = s.logit[some, :]
            hit = s.mask[some, cols] > 0.0
            value = jnp.where(hit, -value, value)
            small = jnp.exp(-jnp.abs(value))
            soft = jnp.maximum(value, 0.0) + jnp.log1p(small)
            over = 1.0 / (1.0 + small)
            under = small * over
            high = value >= 0.0
            chance, rest = jnp.where(high, over, under), jnp.where(high, under, over)
            square = chance * chance
            slope = weight * (square * (chance + 2.0 * rest * soft)) * temper
            s.gl[some, cols] = jnp.where(hit, -slope, slope).astype(BF16)
            return loss + jnp.sum((weight * (square * soft)).reshape(tall // 8, 8, wide), axis=0)

        s.l_part[:, cols] = lax.fori_loop(0, here // tall, row_block, jnp.zeros((8, wide), F32))
        return carry

    lax.fori_loop(0, n_label // wide, label_block, 0)

    def u_z(d):
        return push("u_z", d, s.u_part.at[:, 0, :, rows(next_z(d), d_z)], s.u_rz.at[z], at(next_z(d), y, x))

    def u_x(d):
        return push("u_x", d, s.u_part.at[next_x(d), 1], s.u_rx.at[x], at(z, y, next_x(d)))

    def u_zx(d):
        return push("u_zx", d, s.u_sz.at[next_x(d)], s.u_rzx.at[x], at(z, y, next_x(d)))

    def u_xz(d):
        return push("u_xz", d, s.u_sx.at[:, rows(next_z(d), d_z)], s.u_rxz.at[z], at(next_z(d), y, x))

    def u_block(d):
        cols = rows(next_z(d), d_z)
        part = dot(s.gl[...], s.lh[:, cols])
        s.u_part[:, :, :, cols] = part.astype(BF16).reshape(NX, NY, own, d_z)

    def u_turn(d):
        u_block(d)
        u_z(d).start()

    each(NZ, u_turn)
    sent.append((NZ, u_z))
    u_block(0)
    start(NX, u_x)

    def loss_sum(d):
        return push("loss", d, s.l_part, s.l_recv.at[j], {"lab": next_lab(d)})

    start(NLAB, loss_sum)
    s.l_recv[j] = s.l_part[...]
    arrive(NZ, u_z)
    half = s.u_part[:, 0, :, mine].astype(F32)
    for d in range(1, NZ):
        half += s.u_rz[next_z(d)].astype(F32)
    s.u_sz[...] = half.astype(BF16)
    start(NX, u_zx)
    arrive(NX, u_x)
    half = s.u_part[x, 1].astype(F32)
    for d in range(1, NX):
        half += s.u_rx[next_x(d)].astype(F32)
    s.u_sx[...] = half.astype(BF16)
    start(NZ, u_xz)
    arrive(NX, u_zx)
    half = s.u_sz[x].astype(F32)
    for d in range(1, NX):
        half += s.u_rzx[next_x(d)].astype(F32)
    s.back[0] = half
    arrive(NZ, u_xz)
    half = s.u_sx[:, mine].astype(F32)
    for d in range(1, NZ):
        half += s.u_rxz[next_z(d)].astype(F32)
    s.back[1] = half

    def u_y(d):
        return push("u_y", d, s.back.at[1 - y], s.u_peer, y_peer)

    start(2, u_y)
    arrive(2, u_y)
    s.u[j] = (s.back[y] + s.u_peer[...]).astype(BF16)

    def u_all(d):
        return push("u_all", d, s.u.at[j], s.u.at[j], {"lab": next_lab(d)})

    start(NLAB, u_all)
    arrive(NLAB, u_all)
    u = s.u[...].reshape(block, d_z)

    part = dot(u, s.lp[...].reshape(d_z, width)).reshape(NZ, own, width)
    s.g_part[...] = part
    s.g_send[...] = part.astype(BF16)

    def g_sum(d):
        return push("g_sum", d, s.g_send.at[next_z(d)], s.g_recv.at[z], at(next_z(d), y, x))

    start(NZ, g_sum)
    part = dot(u, s.qe[...].reshape(block, width), ROWS).reshape(NY, NX, d_row, width)
    s.k_part[...] = part
    s.k_send[...] = part.astype(BF16)

    def k_x(d):
        return push("k_x", d, s.k_send.at[:, next_x(d)], s.k_recv.at[x], at(z, y, next_x(d)))

    start(NX, k_x)
    arrive(NZ, g_sum)
    total = s.g_part[z]
    for d in range(1, NZ):
        total += s.g_recv[next_z(d)].astype(F32)
    gqe_out[...] = total
    s.ge[...] = total.astype(BF16)

    def g_bx(d):
        nz, ny = in_b(d)
        return push("g_bx", d, s.ge.at[:, x_cols], s.gx.at[spot_b], at(nz, ny, x))

    def g_bz(d):
        nx, ny = in_c(d)
        return push("g_bz", d, s.ge.at[:, z_cols], s.gz.at[spot_c], at(z, ny, nx))

    start(NZ * NY, g_bx)
    start(NX * NY, g_bz)
    s.gx[spot_b] = s.ge[:, :cut]
    s.gz[spot_c] = s.ge[:, cut:]
    arrive(NLAB, loss_sum)
    losses = jnp.sum(s.l_recv[0] + s.l_recv[1] + s.l_recv[2] + s.l_recv[3], axis=0, keepdims=True)
    loss_out[...] = losses / (NQRY * own)
    arrive(NZ * NY, q_bx)
    arrive(NX * NY, q_bz)

    arrive(NZ * NY, g_bx)
    part = dot(s.qx[...].reshape(here, e_b), s.gx[...].reshape(here, cut), ROWS).reshape(NX, e_row, cut)
    s.px_part[...] = part
    s.px_send[...] = part.astype(BF16)

    def p_x(d):
        return push("p_x", d, s.px_send.at[next_x(d)], s.px_recv.at[x], at(z, y, next_x(d)))

    start(NX, p_x)
    arrive(NX * NY, g_bz)
    part = dot(s.qz[...].reshape(here, e_b), s.gz[...].reshape(here, width - cut), ROWS).reshape(NZ, e_row, width - cut)
    s.pz_part[...] = part
    s.pz_send[...] = part.astype(BF16)

    def p_z(d):
        return push("p_z", d, s.pz_send.at[next_z(d)], s.pz_recv.at[z], at(next_z(d), y, x))

    start(NZ, p_z)

    arrive(NX, k_x)
    total = s.k_part[:, x]
    for d in range(1, NX):
        total += s.k_recv[next_x(d)].astype(F32)
    s.k_sum[...] = total

    def k_y(d):
        return push("k_y", d, s.k_sum.at[1 - y], s.k_peer, y_peer)

    start(2, k_y)
    arrive(NX, p_x)
    total = s.px_part[x]
    for d in range(1, NX):
        total += s.px_recv[next_x(d)].astype(F32)
    gqp_out[:, :cut] = total
    arrive(2, k_y)
    glp_out[...] = s.k_sum[y] + s.k_peer[...]
    arrive(NZ, p_z)
    total = s.pz_part[z]
    for d in range(1, NZ):
        total += s.pz_recv[next_z(d)].astype(F32)
    gqp_out[:, cut:] = total

    for number, copies in sent:
        each(number, lambda d: copies(d).wait_send())
    ids_sent()


class Scratch:
    def __init__(self, names, refs):
        for name, ref in zip(names, refs):
            setattr(self, name, ref)


def shards(query_hidden, query_proj, label_hidden, label_proj, pos_ids, pos_count):
    own, wide_e = query_hidden.shape
    n_label, wide_d = label_hidden.shape
    e_row, width = query_proj.shape
    d_row = label_proj.shape[0]
    slots = pos_ids.shape[1]
    e_z, d_z, e_b = NX * NY * e_row, NX * NY * d_row, NX * e_row
    here = NX * NY * own
    cut = width // 256 * 128
    rest = width - cut
    scratch = {
        "qh": ((own, wide_e), BF16),
        "ids_raw": ((slots, own), jnp.int32),
        "used": ((1, own), jnp.int32),
        "ids_send": ((slots, 128), jnp.int32),
        "ids": ((NX, NY, slots, 128), jnp.int32),
        "lh": ((n_label, wide_d), BF16),
        "lp": ((NY, NX, d_row, width), BF16),
        "wx": ((NY, NX, e_row, cut), BF16),
        "wz": ((NZ, NY, e_row, rest), BF16),
        "q0": ((NZ, own, e_z), BF16),
        "q1_send": ((NX, own, e_z), BF16),
        "q1": ((NX, own, e_z), BF16),
        "qx_send": ((NZ * NY, own, e_b), BF16),
        "qx": ((NZ * NY, own, e_b), BF16),
        "qz_send": ((NX * NY, own, e_b), BF16),
        "qz": ((NX * NY, own, e_b), BF16),
        "part_z": ((NZ, own, cut), F32),
        "sum_z": ((NZ, own, cut), F32),
        "part_x": ((NX, own, rest), F32),
        "sum_x": ((NX, own, rest), F32),
        "mask": ((here, n_label), F32),
        "c_part": ((8, n_label), F32),
        "c_recv": ((NLAB, 8, n_label), F32),
        "weight": ((1, n_label), F32),
        "qe": ((NZ, own, width), BF16),
        "t_part": ((NLAB, own, d_z), F32),
        "t_recv": ((NLAB, own, d_z), F32),
        "t": ((NX, NY, own, wide_d), BF16),
        "logit": ((here, 256), F32),
        "gl": ((here, n_label), BF16),
        "l_part": ((8, n_label), F32),
        "l_recv": ((NLAB, 8, n_label), F32),
        "u_part": ((NX, NY, own, wide_d), BF16),
        "u_rz": ((NZ, NX, own, d_z), BF16),
        "u_rx": ((NX, own, wide_d), BF16),
        "u_sz": ((NX, own, d_z), BF16),
        "u_sx": ((own, wide_d), BF16),
        "u_rzx": ((NX, own, d_z), BF16),
        "u_rxz": ((NZ, own, d_z), BF16),
        "back": ((NY, own, d_z), F32),
        "u_peer": ((own, d_z), F32),
        "u": ((NLAB, own, d_z), BF16),
        "g_part": ((NZ, own, width), F32),
        "g_send": ((NZ, own, width), BF16),
        "g_recv": ((NZ, own, width), BF16),
        "ge": ((own, width), BF16),
        "gx": ((NZ * NY, own, cut), BF16),
        "gz": ((NX * NY, own, rest), BF16),
        "k_part": ((NY, NX, d_row, width), F32),
        "k_send": ((NY, NX, d_row, width), BF16),
        "k_recv": ((NX, NY, d_row, width), BF16),
        "k_sum": ((NY, d_row, width), F32),
        "k_peer": ((d_row, width), F32),
        "px_part": ((NX, e_row, cut), F32),
        "px_send": ((NX, e_row, cut), BF16),
        "px_recv": ((NX, e_row, cut), BF16),
        "pz_part": ((NZ, e_row, rest), F32),
        "pz_send": ((NZ, e_row, rest), BF16),
        "pz_recv": ((NZ, e_row, rest), BF16),
    }
    scratch = {name: pltpu.VMEM(*spec) for name, spec in scratch.items()}
    scratch["load"] = pltpu.SemaphoreType.DMA((7,))
    pairs = ("w_yx", "w_yz", "l_y", "i_y", "t_y", "u_y", "k_y")
    fours = (
        "w_x", "w_z", "w_fx", "w_fz", "q0", "q1", "l_x", "i_x", "i_z", "b_z", "b_x", "count", "q_all", "t_sum",
        "t_x", "t_z", "t_xz", "t_zx", "u_z", "u_x", "u_zx", "u_xz", "loss", "u_all", "g_sum", "k_x", "p_x", "p_z",
    )
    eights = ("q_bx", "q_bz", "g_bx", "g_bz")
    for number, group in ((2, pairs), (4, fours), (8, eights)):
        for name in group:
            scratch["send_" + name] = pltpu.SemaphoreType.DMA((number,))
            scratch["recv_" + name] = pltpu.SemaphoreType.DMA((number,))
    names = tuple(scratch)

    def kernel(*refs):
        step_kernel(wide_e ** (-0.5), cut, *refs[:10], Scratch(names, refs[10:]))

    arrays = [
        pltpu.with_memory_space_constraint(a, pltpu.HBM)
        for a in (query_hidden, query_proj, label_hidden, label_proj, pos_ids.T, pos_count.reshape(1, own))
    ]
    gqp, glp, loss, gqe = pl.pallas_call(
        kernel,
        out_shape=(
            jax.ShapeDtypeStruct((e_row, width), F32),
            jax.ShapeDtypeStruct((d_row, width), F32),
            jax.ShapeDtypeStruct((1, n_label), F32),
            jax.ShapeDtypeStruct((own, width), F32),
        ),
        in_specs=[pl.BlockSpec(memory_space=pltpu.HBM)] * 6,
        out_specs=(pl.BlockSpec(memory_space=pltpu.VMEM),) * 4,
        scratch_shapes=list(scratch.values()),
        compiler_params=pltpu.CompilerParams(
            collective_id=0, has_side_effects=True, vmem_limit_bytes=48 << 20
        ),
        name="focal_step",
    )(*arrays)
    return gqp, glp, loss.reshape(n_label), gqe


def solution(mesh):
    in_specs = (
        P("qry", None),
        P("qry", "lab"),
        P("qry", None),
        P("qry", "lab"),
        P("qry", None),
        P("qry"),
    )
    out_specs = (P("qry", "lab"), P("qry", "lab"), P("qry"), P("qry", "lab"))
    return jax.shard_map(shards, mesh=mesh, in_specs=in_specs, out_specs=out_specs, check_vma=False)
```

```python
import jax
import jax.numpy as jnp
import numpy as np
from jax import lax
from jax.experimental import pallas as pl
from jax.experimental.pallas import tpu as pltpu
from jax.sharding import PartitionSpec as P

NX, NY, NZ, NLAB = 4, 2, 4, 4
NQRY = NX * NY * NZ
ROWS = (((0,), (0,)), ((), ()))
COLS = (((1,), (1,)), ((), ()))
MESH = pl.DeviceIdType.MESH
F32, BF16 = jnp.float32, jnp.bfloat16


def dot(left, right, dims=(((1,), (0,)), ((), ()))):
    return lax.dot_general(left, right, dims, preferred_element_type=F32)


def each(count, step):
    def body(d, carry):
        step(d)
        return carry

    lax.fori_loop(1, count, body, 0)


def step_kernel(temper, cut, qh, qp, lh, lp, ids, used, gqp_out, glp_out, loss_out, gqe_out, s):
    own = qh.shape[0]
    e_row, d_row, width = qp.shape[0], lp.shape[0], qp.shape[1]
    n_label, wide_d = lh.shape
    e_z, d_z = NX * NY * e_row, NX * NY * d_row
    e_b = NX * e_row
    here, block = NX * NY * own, NZ * own
    me, j = lax.axis_index("qry"), lax.axis_index("lab")
    x, y, z = lax.rem(me, NX), lax.rem(lax.div(me, NX), NY), lax.div(me, NX * NY)

    def at(nz, ny, nx):
        return {"qry": (nz * NY + ny) * NX + nx}

    y_peer = at(z, 1 - y, x)

    def next_x(d):
        return lax.rem(x + d, NX)

    def next_z(d):
        return lax.rem(z + d, NZ)

    def next_lab(d):
        return lax.rem(j + d, NLAB)

    def across(d):
        return {**y_peer, "lab": next_lab(d)}

    def rows(index, size):
        return pl.ds(pl.multiple_of(index * size, size), size)

    def push(name, d, src, dst, device):
        return pltpu.make_async_remote_copy(
            src_ref=src,
            dst_ref=dst,
            send_sem=getattr(s, "send_" + name).at[d],
            recv_sem=getattr(s, "recv_" + name).at[d],
            device_id=device,
            device_id_type=MESH,
        )

    sent = []

    def start(count, copies):
        each(count, lambda d: copies(d).start())
        sent.append((count, copies))

    def arrive(count, copies):
        each(count, lambda d: copies(d).wait_recv())

    loads = [
        pltpu.make_async_copy(source, target, s.load.at[k])
        for k, (source, target) in enumerate(
            (
                (qh, s.qh),
                (ids, s.ids_raw),
                (used, s.used),
                (qp.at[:, pl.ds(0, cut)], s.wx.at[y, x]),
                (qp.at[:, pl.ds(cut, width - cut)], s.wz.at[z, y]),
                (lp, s.lp.at[y, x]),
                (lh, s.lh),
            )
        )
    ]
    for load in loads:
        load.start()

    barrier = pltpu.get_barrier_semaphore()

    def greet(device):
        pl.semaphore_signal(barrier, inc=1, device_id=device, device_id_type=MESH)

    each(NX, lambda d: greet(at(z, y, next_x(d))))
    each(NZ, lambda d: greet(at(next_z(d), y, x)))
    greet(y_peer)
    each(NX, lambda d: greet(at(z, 1 - y, next_x(d))))
    each(NZ, lambda d: greet(at(next_z(d), 1 - y, x)))
    each(NLAB, lambda d: greet({"lab": next_lab(d)}))
    each(NLAB, lambda d: greet(across(d)))

    loads[0].wait()
    for k in range(NX):
        s.q1_send[k] = jnp.concatenate(
            [s.qh[:, (NX * r + k) * e_row : (NX * r + k + 1) * e_row] for r in range(NZ * NY)], axis=1
        )
    for k in range(NZ * NY):
        s.qx_send[k] = s.qh[:, k * e_b : (k + 1) * e_b]
    for nx in range(NX):
        for ny in range(NY):
            first = [(NX * (NY * r + ny) + nx) * e_row for r in range(NZ)]
            s.qz_send[NY * nx + ny] = jnp.concatenate([s.qh[:, f : f + e_row] for f in first], axis=1)
    loads[1].wait()
    loads[2].wait()
    slots = ids.shape[0]
    s.ids_send[...] = jnp.full(s.ids_send.shape, -1, jnp.int32)
    slot_at = lax.broadcasted_iota(jnp.int32, ids.shape, 0)
    s.ids_send[:, :own] = jnp.where(slot_at < s.used[...], s.ids_raw[...], -1)
    pl.semaphore_wait(barrier, 2 * (NX - 1) + 2 * (NZ - 1) + 1 + 2 * (NLAB - 1))

    x_cols, z_cols = pl.ds(0, cut), pl.ds(cut, width - cut)

    def w_yx(d):
        return push("w_yx", d, qp.at[:, x_cols], s.wx.at[y, x], y_peer)

    def w_yz(d):
        return push("w_yz", d, qp.at[:, z_cols], s.wz.at[z, y], y_peer)

    def w_x(d):
        return push("w_x", d, qp.at[:, x_cols], s.wx.at[y, x], at(z, y, next_x(d)))

    def w_z(d):
        return push("w_z", d, qp.at[:, z_cols], s.wz.at[z, y], at(next_z(d), y, x))

    def w_fx(d):
        return push("w_fx", d, s.wx.at[1 - y, x], s.wx.at[1 - y, x], at(z, y, next_x(d)))

    def w_fz(d):
        return push("w_fz", d, s.wz.at[z, 1 - y], s.wz.at[z, 1 - y], at(next_z(d), y, x))

    def q0(d):
        return push("q0", d, qh.at[:, rows(next_z(d), e_z)], s.q0.at[z], at(next_z(d), y, x))

    def q1(d):
        return push("q1", d, s.q1_send.at[next_x(d)], s.q1.at[x], at(z, y, next_x(d)))

    def l_x(d):
        return push("l_x", d, lp, s.lp.at[y, x], at(z, y, next_x(d)))

    def l_own(d):
        return push("l_own", d, lp, s.lp.at[y, x], y_peer)

    def l_y(d):
        block_at = s.lp.at[y, lax.rem(x + NX - d, NX)]
        return push("l_y", d, block_at, block_at, y_peer)

    start(NX, l_x)
    start(2, w_yx)
    start(2, w_yz)
    start(2, l_own)
    start(NX, w_x)
    start(NZ, w_z)
    start(NZ, q0)
    start(NX, q1)

    def i_y(d):
        return push("i_y", d, s.ids_send, s.ids.at[x, y], y_peer)

    def i_x(d):
        return push("i_x", d, s.ids.at[x], s.ids.at[x], at(z, y, next_x(d)))

    def i_z(d):
        return push("i_z", d, s.ids, s.ids, at(next_z(d), y, x))

    holder = z == j

    @pl.when(holder)
    def _():
        i_y(1).start()
        s.ids[x, y] = s.ids_send[...]
        i_y(1).wait_recv()
        each(NX, lambda d: i_x(d).start())

    s.q0[z] = s.qh[:, rows(z, e_z)]
    s.q1[x] = s.q1_send[x]
    arrive(2, w_yx)
    start(NX, w_fx)
    arrive(2, w_yz)
    start(NZ, w_fz)

    @pl.when(holder)
    def _():
        arrive(NX, i_x)
        each(NZ, lambda d: i_z(d).start())

    def ids_arrive():
        @pl.when(jnp.logical_not(holder))
        def _():
            i_z(lax.rem(z - j + NZ, NZ)).wait_recv()

    def ids_sent():
        @pl.when(holder)
        def _():
            i_y(1).wait_send()
            each(NX, lambda d: i_x(d).wait_send())
            each(NZ, lambda d: i_z(d).wait_send())

    arrive(NX, l_x)
    start(NX, l_y)

    arrive(NZ, q0)
    arrive(NX, w_x)
    loads[3].wait()
    arrive(NX, w_fx)
    s.part_z[...] = dot(s.q0[...].reshape(block, e_z), s.wx[...].reshape(e_z, cut)).reshape(NZ, own, cut)

    def b_z(d):
        return push("b_z", d, s.part_z.at[next_z(d)], s.sum_z.at[z], at(next_z(d), y, x))

    start(NZ, b_z)
    arrive(NX, q1)
    arrive(NZ, w_z)
    loads[4].wait()
    arrive(NZ, w_fz)
    s.part_x[...] = dot(s.q1[...].reshape(block, e_z), s.wz[...].reshape(e_z, width - cut)).reshape(NX, own, width - cut)

    def b_x(d):
        return push("b_x", d, s.part_x.at[next_x(d)], s.sum_x.at[x], at(z, y, next_x(d)))

    start(NX, b_x)
    s.sum_z[z] = s.part_z[z]
    s.sum_x[x] = s.part_x[x]

    ids_arrive()
    local = s.ids[...].reshape(NX * NY * slots, s.ids.shape[3]).T - n_label * me
    wide = 256
    for c in range(n_label // wide):
        column = lax.broadcasted_iota(jnp.int32, (own, wide), 1) + c * wide
        tally = jnp.zeros((8, wide), F32)
        for k in range(NX * NY):
            found = jnp.zeros((own, wide), F32)
            for slot in range(k * slots, (k + 1) * slots):
                found += jnp.where(local[:own, slot : slot + 1] == column, 1.0, 0.0)
            s.mask[k * own : (k + 1) * own, c * wide : (c + 1) * wide] = found
            tally += jnp.sum(found.reshape(own // 8, 8, wide), axis=0)
        s.c_part[:, c * wide : (c + 1) * wide] = tally

    def count(d):
        return push("count", d, s.c_part, s.c_recv.at[j], {"lab": next_lab(d)})

    start(NLAB, count)
    s.c_recv[j] = s.c_part[...]

    arrive(NZ, b_z)
    s.qe[z, :, :cut] = (s.sum_z[0] + s.sum_z[1] + s.sum_z[2] + s.sum_z[3]).astype(BF16)
    arrive(NX, b_x)
    s.qe[z, :, cut:] = (s.sum_x[0] + s.sum_x[1] + s.sum_x[2] + s.sum_x[3]).astype(BF16)

    def q_all(d):
        return push("q_all", d, s.qe.at[z], s.qe.at[z], at(next_z(d), y, x))

    start(NZ, q_all)
    loads[5].wait()
    arrive(2, l_own)
    arrive(NX, l_y)
    arrive(NZ, q_all)

    part = dot(s.qe[...].reshape(block, width), s.lp[...].reshape(d_z, width), COLS)
    s.t_part[...] = part.astype(BF16).reshape(NLAB, own, d_z)

    def t_sum(d):
        return push("t_sum", d, s.t_part.at[next_lab(d)], s.t_recv.at[y, j], {"lab": next_lab(d)})

    def t_cross(d):
        return push("t_cross", d, s.t_part.at[next_lab(d)], s.t_recv.at[y, j], across(d))

    start(NLAB, t_sum)
    start(NLAB + 1, t_cross)
    s.t_recv[y, j] = s.t_part[j]

    arrive(NLAB, count)
    counts = jnp.sum(s.c_recv[0] + s.c_recv[1] + s.c_recv[2] + s.c_recv[3], axis=0, keepdims=True)
    s.weight[...] = (1.0 - 0.99) / (1.0 - jnp.exp((counts + 1.0) * float(np.log(np.float64(np.float32(0.99))))))

    arrive(NLAB, t_sum)
    arrive(NLAB + 1, t_cross)
    mine = rows(z, d_z)
    total = s.t_recv[:, 0].astype(F32)
    for k in range(1, NLAB):
        total += s.t_recv[:, k].astype(F32)
    s.t[x, :, :, mine] = total.astype(BF16)

    def t_x(d):
        return push("t_x", d, s.t.at[x, 0, :, mine], s.t.at[x, 0, :, mine], at(z, y, next_x(d)))

    def t_z(d):
        return push("t_z", d, s.t.at[x, 1, :, mine], s.t.at[x, 1, :, mine], at(next_z(d), y, x))

    def t_xz(d):
        return push("t_xz", d, s.t.at[:, 0, :, mine], s.t.at[:, 0, :, mine], at(next_z(d), y, x))

    def t_zx(d):
        return push("t_zx", d, s.t.at[x, 1], s.t.at[x, 1], at(z, y, next_x(d)))

    start(NX, t_x)
    start(NZ, t_z)
    arrive(NX, t_x)
    start(NZ, t_xz)
    arrive(NZ, t_z)
    start(NX, t_zx)
    loads[6].wait()
    arrive(NZ, t_xz)
    arrive(NX, t_zx)

    def in_b(d):
        return lax.rem(z + lax.div(d, NY), NZ), lax.rem(y + lax.rem(d, NY), NY)

    def in_c(d):
        return lax.rem(x + lax.div(d, NY), NX), lax.rem(y + lax.rem(d, NY), NY)

    spot_b, spot_c = NY * z + y, NY * x + y

    def q_bx(d):
        nz, ny = in_b(d)
        return push("q_bx", d, s.qx_send.at[NY * nz + ny], s.qx.at[spot_b], at(nz, ny, x))

    def q_bz(d):
        nx, ny = in_c(d)
        return push("q_bz", d, s.qz_send.at[NY * nx + ny], s.qz.at[spot_c], at(z, ny, nx))

    start(NZ * NY, q_bx)
    start(NX * NY, q_bz)
    s.qx[spot_b] = s.qx_send[spot_b]
    s.qz[spot_c] = s.qz_send[spot_c]

    tall = 32

    def label_block(c, carry):
        cols = rows(c, wide)
        s.logit[...] = dot(s.t[...].reshape(here, wide_d), s.lh[cols, :], COLS) * temper
        weight = s.weight[:, cols]

        def row_block(r, loss):
            some = rows(r, tall)
            value = s.logit[some, :]
            hit = s.mask[some, cols] > 0.0
            value = jnp.where(hit, -value, value)
            small = jnp.exp(-jnp.abs(value))
            soft = jnp.maximum(value, 0.0) + jnp.log1p(small)
            over = 1.0 / (1.0 + small)
            under = small * over
            high = value >= 0.0
            chance, rest = jnp.where(high, over, under), jnp.where(high, under, over)
            square = chance * chance
            slope = weight * (square * (chance + 2.0 * rest * soft)) * temper
            s.gl[some, cols] = jnp.where(hit, -slope, slope).astype(BF16)
            return loss + jnp.sum((weight * (square * soft)).reshape(tall // 8, 8, wide), axis=0)

        s.l_part[:, cols] = lax.fori_loop(0, here // tall, row_block, jnp.zeros((8, wide), F32))
        return carry

    lax.fori_loop(0, n_label // wide, label_block, 0)

    def u_z(d):
        return push("u_z", d, s.u_part.at[:, 0, :, rows(next_z(d), d_z)], s.u_rz.at[z], at(next_z(d), y, x))

    def u_x(d):
        return push("u_x", d, s.u_part.at[next_x(d), 1], s.u_rx.at[x], at(z, y, next_x(d)))

    def u_zx(d):
        return push("u_zx", d, s.u_sz.at[next_x(d)], s.u_rzx.at[x], at(z, y, next_x(d)))

    def u_xz(d):
        return push("u_xz", d, s.u_sx.at[:, rows(next_z(d), d_z)], s.u_rxz.at[z], at(next_z(d), y, x))

    def u_block(d):
        cols = rows(next_z(d), d_z)
        part = dot(s.gl[...], s.lh[:, cols])
        s.u_part[:, :, :, cols] = part.astype(BF16).reshape(NX, NY, own, d_z)

    def u_turn(d):
        u_block(d)
        u_z(d).start()

    each(NZ, u_turn)
    sent.append((NZ, u_z))
    u_block(0)
    start(NX, u_x)

    def loss_sum(d):
        return push("loss", d, s.l_part, s.l_recv.at[j], {"lab": next_lab(d)})

    start(NLAB, loss_sum)
    s.l_recv[j] = s.l_part[...]
    arrive(NZ, u_z)
    half = s.u_part[:, 0, :, mine].astype(F32)
    for d in range(1, NZ):
        half += s.u_rz[next_z(d)].astype(F32)
    s.u_sz[...] = half.astype(BF16)
    start(NX, u_zx)
    arrive(NX, u_x)
    half = s.u_part[x, 1].astype(F32)
    for d in range(1, NX):
        half += s.u_rx[next_x(d)].astype(F32)
    s.u_sx[...] = half.astype(BF16)
    start(NZ, u_xz)
    arrive(NX, u_zx)
    half = s.u_sz[x].astype(F32)
    for d in range(1, NX):
        half += s.u_rzx[next_x(d)].astype(F32)
    s.back[0] = half
    arrive(NZ, u_xz)
    half = s.u_sx[:, mine].astype(F32)
    for d in range(1, NZ):
        half += s.u_rxz[next_z(d)].astype(F32)
    s.back[1] = half

    s.u_send[...] = s.back[...].astype(BF16)

    def u_all(d):
        return push("u_all", d, s.u_send.at[y], s.u.at[y, j], {"lab": next_lab(d)})

    def u_cross(d):
        return push("u_cross", d, s.u_send.at[1 - y], s.u.at[y, j], across(d))

    start(NLAB, u_all)
    start(NLAB + 1, u_cross)
    s.u[y, j] = s.u_send[y]
    arrive(NLAB, u_all)
    arrive(NLAB + 1, u_cross)
    u = [s.u[k].reshape(block, d_z) for k in range(NY)]

    l_proj = s.lp[...].reshape(d_z, width)
    part = (dot(u[0], l_proj) + dot(u[1], l_proj)).reshape(NZ, own, width)
    s.g_part[...] = part
    s.g_send[...] = part.astype(BF16)

    def g_sum(d):
        return push("g_sum", d, s.g_send.at[next_z(d)], s.g_recv.at[z], at(next_z(d), y, x))

    start(NZ, g_sum)
    qe = s.qe[...].reshape(block, width)
    part = (dot(u[0], qe, ROWS) + dot(u[1], qe, ROWS)).reshape(NY, NX, d_row, width)
    s.k_part[...] = part
    s.k_send[...] = part.astype(BF16)

    def k_x(d):
        return push("k_x", d, s.k_send.at[:, next_x(d)], s.k_recv.at[x], at(z, y, next_x(d)))

    start(NX, k_x)
    arrive(NZ, g_sum)
    total = s.g_part[z]
    for d in range(1, NZ):
        total += s.g_recv[next_z(d)].astype(F32)
    gqe_out[...] = total
    s.ge[...] = total.astype(BF16)

    def g_yx(d):
        return push("g_yx", d, s.ge.at[:, x_cols], s.gx.at[spot_b], y_peer)

    def g_yz(d):
        return push("g_yz", d, s.ge.at[:, z_cols], s.gz.at[spot_c], y_peer)

    def g_z(d):
        return push("g_z", d, s.ge.at[:, x_cols], s.gx.at[spot_b], at(next_z(d), y, x))

    def g_x(d):
        return push("g_x", d, s.ge.at[:, z_cols], s.gz.at[spot_c], at(z, y, next_x(d)))

    def g_fz(d):
        other = s.gx.at[NY * z + 1 - y]
        return push("g_fz", d, other, other, at(next_z(d), y, x))

    def g_fx(d):
        other = s.gz.at[NY * x + 1 - y]
        return push("g_fx", d, other, other, at(z, y, next_x(d)))

    start(2, g_yx)
    start(2, g_yz)
    start(NZ, g_z)
    start(NX, g_x)
    arrive(2, g_yx)
    start(NZ, g_fz)
    arrive(2, g_yz)
    start(NX, g_fx)
    s.gx[spot_b] = s.ge[:, :cut]
    s.gz[spot_c] = s.ge[:, cut:]
    arrive(NLAB, loss_sum)
    losses = jnp.sum(s.l_recv[0] + s.l_recv[1] + s.l_recv[2] + s.l_recv[3], axis=0, keepdims=True)
    loss_out[...] = losses / (NQRY * own)
    arrive(NZ * NY, q_bx)
    arrive(NX * NY, q_bz)

    arrive(NZ, g_z)
    arrive(NZ, g_fz)
    part = dot(s.qx[...].reshape(here, e_b), s.gx[...].reshape(here, cut), ROWS).reshape(NX, e_row, cut)
    s.px_part[...] = part
    s.px_send[...] = part.astype(BF16)

    def p_x(d):
        return push("p_x", d, s.px_send.at[next_x(d)], s.px_recv.at[x], at(z, y, next_x(d)))

    start(NX, p_x)
    arrive(NX, g_x)
    arrive(NX, g_fx)
    part = dot(s.qz[...].reshape(here, e_b), s.gz[...].reshape(here, width - cut), ROWS).reshape(NZ, e_row, width - cut)
    s.pz_part[...] = part
    s.pz_send[...] = part.astype(BF16)

    def p_z(d):
        return push("p_z", d, s.pz_send.at[next_z(d)], s.pz_recv.at[z], at(next_z(d), y, x))

    start(NZ, p_z)

    arrive(NX, k_x)
    total = s.k_part[:, x]
    for d in range(1, NX):
        total += s.k_recv[next_x(d)].astype(F32)
    s.k_sum[...] = total

    def k_y(d):
        return push("k_y", d, s.k_sum.at[1 - y], s.k_peer, y_peer)

    start(2, k_y)
    arrive(NX, p_x)
    total = s.px_part[x]
    for d in range(1, NX):
        total += s.px_recv[next_x(d)].astype(F32)
    gqp_out[:, :cut] = total
    arrive(2, k_y)
    glp_out[...] = s.k_sum[y] + s.k_peer[...]
    arrive(NZ, p_z)
    total = s.pz_part[z]
    for d in range(1, NZ):
        total += s.pz_recv[next_z(d)].astype(F32)
    gqp_out[:, cut:] = total

    for number, copies in sent:
        each(number, lambda d: copies(d).wait_send())
    ids_sent()


class Scratch:
    def __init__(self, names, refs):
        for name, ref in zip(names, refs):
            setattr(self, name, ref)


def shards(query_hidden, query_proj, label_hidden, label_proj, pos_ids, pos_count):
    own, wide_e = query_hidden.shape
    n_label, wide_d = label_hidden.shape
    e_row, width = query_proj.shape
    d_row = label_proj.shape[0]
    slots = pos_ids.shape[1]
    e_z, d_z, e_b = NX * NY * e_row, NX * NY * d_row, NX * e_row
    here = NX * NY * own
    cut = width // 256 * 128
    rest = width - cut
    scratch = {
        "qh": ((own, wide_e), BF16),
        "ids_raw": ((slots, own), jnp.int32),
        "used": ((1, own), jnp.int32),
        "ids_send": ((slots, 128), jnp.int32),
        "ids": ((NX, NY, slots, 128), jnp.int32),
        "lh": ((n_label, wide_d), BF16),
        "lp": ((NY, NX, d_row, width), BF16),
        "wx": ((NY, NX, e_row, cut), BF16),
        "wz": ((NZ, NY, e_row, rest), BF16),
        "q0": ((NZ, own, e_z), BF16),
        "q1_send": ((NX, own, e_z), BF16),
        "q1": ((NX, own, e_z), BF16),
        "qx_send": ((NZ * NY, own, e_b), BF16),
        "qx": ((NZ * NY, own, e_b), BF16),
        "qz_send": ((NX * NY, own, e_b), BF16),
        "qz": ((NX * NY, own, e_b), BF16),
        "part_z": ((NZ, own, cut), F32),
        "sum_z": ((NZ, own, cut), F32),
        "part_x": ((NX, own, rest), F32),
        "sum_x": ((NX, own, rest), F32),
        "mask": ((here, n_label), F32),
        "c_part": ((8, n_label), F32),
        "c_recv": ((NLAB, 8, n_label), F32),
        "weight": ((1, n_label), F32),
        "qe": ((NZ, own, width), BF16),
        "t_part": ((NLAB, own, d_z), BF16),
        "t_recv": ((NY, NLAB, own, d_z), BF16),
        "t": ((NX, NY, own, wide_d), BF16),
        "logit": ((here, 256), F32),
        "gl": ((here, n_label), BF16),
        "l_part": ((8, n_label), F32),
        "l_recv": ((NLAB, 8, n_label), F32),
        "u_part": ((NX, NY, own, wide_d), BF16),
        "u_rz": ((NZ, NX, own, d_z), BF16),
        "u_rx": ((NX, own, wide_d), BF16),
        "u_sz": ((NX, own, d_z), BF16),
        "u_sx": ((own, wide_d), BF16),
        "u_rzx": ((NX, own, d_z), BF16),
        "u_rxz": ((NZ, own, d_z), BF16),
        "back": ((NY, own, d_z), F32),
        "u_send": ((NY, own, d_z), BF16),
        "u": ((NY, NLAB, own, d_z), BF16),
        "g_part": ((NZ, own, width), F32),
        "g_send": ((NZ, own, width), BF16),
        "g_recv": ((NZ, own, width), BF16),
        "ge": ((own, width), BF16),
        "gx": ((NZ * NY, own, cut), BF16),
        "gz": ((NX * NY, own, rest), BF16),
        "k_part": ((NY, NX, d_row, width), F32),
        "k_send": ((NY, NX, d_row, width), BF16),
        "k_recv": ((NX, NY, d_row, width), BF16),
        "k_sum": ((NY, d_row, width), F32),
        "k_peer": ((d_row, width), F32),
        "px_part": ((NX, e_row, cut), F32),
        "px_send": ((NX, e_row, cut), BF16),
        "px_recv": ((NX, e_row, cut), BF16),
        "pz_part": ((NZ, e_row, rest), F32),
        "pz_send": ((NZ, e_row, rest), BF16),
        "pz_recv": ((NZ, e_row, rest), BF16),
    }
    scratch = {name: pltpu.VMEM(*spec) for name, spec in scratch.items()}
    scratch["load"] = pltpu.SemaphoreType.DMA((7,))
    pairs = ("w_yx", "w_yz", "l_own", "i_y", "g_yx", "g_yz", "k_y")
    fours = (
        "w_x", "w_z", "w_fx", "w_fz", "q0", "q1", "l_x", "l_y", "i_x", "i_z", "b_z", "b_x", "count", "q_all", "t_sum",
        "t_x", "t_z", "t_xz", "t_zx", "u_z", "u_x", "u_zx", "u_xz", "loss", "u_all", "g_sum", "g_z", "g_x", "g_fz", "g_fx", "k_x", "p_x", "p_z",
    )
    fives, eights = ("t_cross", "u_cross"), ("q_bx", "q_bz")
    for number, group in ((2, pairs), (4, fours), (5, fives), (8, eights)):
        for name in group:
            scratch["send_" + name] = pltpu.SemaphoreType.DMA((number,))
            scratch["recv_" + name] = pltpu.SemaphoreType.DMA((number,))
    names = tuple(scratch)

    def kernel(*refs):
        step_kernel(wide_e ** (-0.5), cut, *refs[:10], Scratch(names, refs[10:]))

    arrays = [
        pltpu.with_memory_space_constraint(a, pltpu.HBM)
        for a in (query_hidden, query_proj, label_hidden, label_proj, pos_ids.T, pos_count.reshape(1, own))
    ]
    gqp, glp, loss, gqe = pl.pallas_call(
        kernel,
        out_shape=(
            jax.ShapeDtypeStruct((e_row, width), F32),
            jax.ShapeDtypeStruct((d_row, width), F32),
            jax.ShapeDtypeStruct((1, n_label), F32),
            jax.ShapeDtypeStruct((own, width), F32),
        ),
        in_specs=[pl.BlockSpec(memory_space=pltpu.HBM)] * 6,
        out_specs=(pl.BlockSpec(memory_space=pltpu.VMEM),) * 4,
        scratch_shapes=list(scratch.values()),
        compiler_params=pltpu.CompilerParams(
            collective_id=0, has_side_effects=True, vmem_limit_bytes=48 << 20
        ),
        name="focal_step",
    )(*arrays)
    return gqp, glp, loss.reshape(n_label), gqe


def solution(mesh):
    in_specs = (
        P("qry", None),
        P("qry", "lab"),
        P("qry", None),
        P("qry", "lab"),
        P("qry", None),
        P("qry"),
    )
    out_specs = (P("qry", "lab"), P("qry", "lab"), P("qry"), P("qry", "lab"))
    return jax.shard_map(shards, mesh=mesh, in_specs=in_specs, out_specs=out_specs, check_vma=False)
```

```python
import jax
import jax.numpy as jnp
import numpy as np
from jax import lax
from jax.experimental import pallas as pl
from jax.experimental.pallas import tpu as pltpu
from jax.sharding import PartitionSpec as P

NX, NY, NZ, NLAB = 4, 2, 4, 4
NQRY = NX * NY * NZ
ROWS = (((0,), (0,)), ((), ()))
COLS = (((1,), (1,)), ((), ()))
MESH = pl.DeviceIdType.MESH
F32, BF16 = jnp.float32, jnp.bfloat16


def dot(left, right, dims=(((1,), (0,)), ((), ()))):
    return lax.dot_general(left, right, dims, preferred_element_type=F32)


def each(count, step):
    def body(d, carry):
        step(d)
        return carry

    lax.fori_loop(1, count, body, 0)


def step_kernel(temper, cut, qh, qp, lh, lp, ids, used, gqp_out, glp_out, loss_out, gqe_out, s):
    own = qh.shape[0]
    e_row, d_row, width = qp.shape[0], lp.shape[0], qp.shape[1]
    n_label, wide_d = lh.shape
    e_z, d_z = NX * NY * e_row, NX * NY * d_row
    e_b = NX * e_row
    here, block = NX * NY * own, NZ * own
    me, j = lax.axis_index("qry"), lax.axis_index("lab")
    x, y, z = lax.rem(me, NX), lax.rem(lax.div(me, NX), NY), lax.div(me, NX * NY)

    def at(nz, ny, nx):
        return {"qry": (nz * NY + ny) * NX + nx}

    y_peer = at(z, 1 - y, x)

    def next_x(d):
        return lax.rem(x + d, NX)

    def next_z(d):
        return lax.rem(z + d, NZ)

    def next_lab(d):
        return lax.rem(j + d, NLAB)

    def across(d):
        return {**y_peer, "lab": next_lab(d)}

    def rows(index, size):
        return pl.ds(pl.multiple_of(index * size, size), size)

    def push(name, d, src, dst, device):
        return pltpu.make_async_remote_copy(
            src_ref=src,
            dst_ref=dst,
            send_sem=getattr(s, "send_" + name).at[d],
            recv_sem=getattr(s, "recv_" + name).at[d],
            device_id=device,
            device_id_type=MESH,
        )

    sent = []

    def start(count, copies):
        each(count, lambda d: copies(d).start())
        sent.append((count, copies))

    def arrive(count, copies):
        each(count, lambda d: copies(d).wait_recv())

    loads = [
        pltpu.make_async_copy(source, target, s.load.at[k])
        for k, (source, target) in enumerate(
            (
                (qh, s.qh),
                (ids, s.ids_raw),
                (used, s.used),
                (qp.at[:, pl.ds(0, cut)], s.wx.at[y, x]),
                (qp.at[:, pl.ds(cut, width - cut)], s.wz.at[z, y]),
                (lp, s.lp.at[y, x]),
                (lh, s.lh),
            )
        )
    ]
    for load in loads:
        load.start()

    barrier = pltpu.get_barrier_semaphore()

    def greet(device):
        pl.semaphore_signal(barrier, inc=1, device_id=device, device_id_type=MESH)

    each(NX, lambda d: greet(at(z, y, next_x(d))))
    each(NZ, lambda d: greet(at(next_z(d), y, x)))
    greet(y_peer)
    each(NX, lambda d: greet(at(z, 1 - y, next_x(d))))
    each(NZ, lambda d: greet(at(next_z(d), 1 - y, x)))
    each(NLAB, lambda d: greet({"lab": next_lab(d)}))
    each(NLAB, lambda d: greet(across(d)))

    loads[0].wait()
    for k in range(NX):
        s.q1_send[k] = jnp.concatenate(
            [s.qh[:, (NX * r + k) * e_row : (NX * r + k + 1) * e_row] for r in range(NZ * NY)], axis=1
        )
    for k in range(NZ * NY):
        s.qx_send[k] = s.qh[:, k * e_b : (k + 1) * e_b]
    for nx in range(NX):
        for ny in range(NY):
            first = [(NX * (NY * r + ny) + nx) * e_row for r in range(NZ)]
            s.qz_send[NY * nx + ny] = jnp.concatenate([s.qh[:, f : f + e_row] for f in first], axis=1)
    loads[1].wait()
    loads[2].wait()
    slots = ids.shape[0]
    s.ids_send[...] = jnp.full(s.ids_send.shape, -1, jnp.int32)
    slot_at = lax.broadcasted_iota(jnp.int32, ids.shape, 0)
    s.ids_send[:, :own] = jnp.where(slot_at < s.used[...], s.ids_raw[...], -1)
    pl.semaphore_wait(barrier, 2 * (NX - 1) + 2 * (NZ - 1) + 1 + 2 * (NLAB - 1))

    x_cols, z_cols = pl.ds(0, cut), pl.ds(cut, width - cut)

    def w_yx(d):
        return push("w_yx", d, qp.at[:, x_cols], s.wx.at[y, x], y_peer)

    def w_yz(d):
        return push("w_yz", d, qp.at[:, z_cols], s.wz.at[z, y], y_peer)

    def w_x(d):
        return push("w_x", d, qp.at[:, x_cols], s.wx.at[y, x], at(z, y, next_x(d)))

    def w_z(d):
        return push("w_z", d, qp.at[:, z_cols], s.wz.at[z, y], at(next_z(d), y, x))

    def w_fx(d):
        return push("w_fx", d, s.wx.at[1 - y, x], s.wx.at[1 - y, x], at(z, y, next_x(d)))

    def w_fz(d):
        return push("w_fz", d, s.wz.at[z, 1 - y], s.wz.at[z, 1 - y], at(next_z(d), y, x))

    def q0(d):
        return push("q0", d, qh.at[:, rows(next_z(d), e_z)], s.q0.at[z], at(next_z(d), y, x))

    def q1(d):
        return push("q1", d, s.q1_send.at[next_x(d)], s.q1.at[x], at(z, y, next_x(d)))

    def l_x(d):
        return push("l_x", d, lp, s.lp.at[y, x], at(z, y, next_x(d)))

    def l_own(d):
        return push("l_own", d, lp, s.lp.at[y, x], y_peer)

    def l_y(d):
        block_at = s.lp.at[y, lax.rem(x + NX - d, NX)]
        return push("l_y", d, block_at, block_at, y_peer)

    start(NX, l_x)
    start(2, w_yx)
    start(2, w_yz)
    start(2, l_own)
    start(NX, w_x)
    start(NZ, w_z)
    start(NZ, q0)
    start(NX, q1)

    def i_y(d):
        return push("i_y", d, s.ids_send, s.ids.at[x, y], y_peer)

    def i_x(d):
        return push("i_x", d, s.ids.at[x], s.ids.at[x], at(z, y, next_x(d)))

    def i_z(d):
        return push("i_z", d, s.ids, s.ids, at(next_z(d), y, x))

    holder = z == j

    @pl.when(holder)
    def _():
        i_y(1).start()
        s.ids[x, y] = s.ids_send[...]
        i_y(1).wait_recv()
        each(NX, lambda d: i_x(d).start())

    s.q0[z] = s.qh[:, rows(z, e_z)]
    s.q1[x] = s.q1_send[x]
    arrive(2, w_yx)
    start(NX, w_fx)
    arrive(2, w_yz)
    start(NZ, w_fz)

    @pl.when(holder)
    def _():
        arrive(NX, i_x)
        each(NZ, lambda d: i_z(d).start())

    def ids_arrive():
        @pl.when(jnp.logical_not(holder))
        def _():
            i_z(lax.rem(z - j + NZ, NZ)).wait_recv()

    def ids_sent():
        @pl.when(holder)
        def _():
            i_y(1).wait_send()
            each(NX, lambda d: i_x(d).wait_send())
            each(NZ, lambda d: i_z(d).wait_send())

    arrive(NX, l_x)
    start(NX, l_y)

    arrive(NZ, q0)
    arrive(NX, w_x)
    loads[3].wait()
    arrive(NX, w_fx)
    s.part_z[...] = dot(s.q0[...].reshape(block, e_z), s.wx[...].reshape(e_z, cut)).reshape(NZ, own, cut)

    def b_z(d):
        return push("b_z", d, s.part_z.at[next_z(d)], s.sum_z.at[z], at(next_z(d), y, x))

    start(NZ, b_z)
    arrive(NX, q1)
    arrive(NZ, w_z)
    loads[4].wait()
    arrive(NZ, w_fz)
    s.part_x[...] = dot(s.q1[...].reshape(block, e_z), s.wz[...].reshape(e_z, width - cut)).reshape(NX, own, width - cut)

    def b_x(d):
        return push("b_x", d, s.part_x.at[next_x(d)], s.sum_x.at[x], at(z, y, next_x(d)))

    start(NX, b_x)
    s.sum_z[z] = s.part_z[z]
    s.sum_x[x] = s.part_x[x]

    ids_arrive()
    local = s.ids[...].reshape(NX * NY * slots, s.ids.shape[3]).T - n_label * me
    wide = 256
    for c in range(n_label // wide):
        column = lax.broadcasted_iota(jnp.int32, (own, wide), 1) + c * wide
        tally = jnp.zeros((8, wide), F32)
        for k in range(NX * NY):
            found = jnp.zeros((own, wide), F32)
            for slot in range(k * slots, (k + 1) * slots):
                found += jnp.where(local[:own, slot : slot + 1] == column, 1.0, 0.0)
            s.mask[k * own : (k + 1) * own, c * wide : (c + 1) * wide] = found
            tally += jnp.sum(found.reshape(own // 8, 8, wide), axis=0)
        s.c_part[:, c * wide : (c + 1) * wide] = tally

    def count(d):
        return push("count", d, s.c_part, s.c_recv.at[j], {"lab": next_lab(d)})

    start(NLAB, count)
    s.c_recv[j] = s.c_part[...]

    arrive(NZ, b_z)
    s.qe[z, :, :cut] = (s.sum_z[0] + s.sum_z[1] + s.sum_z[2] + s.sum_z[3]).astype(BF16)
    arrive(NX, b_x)
    s.qe[z, :, cut:] = (s.sum_x[0] + s.sum_x[1] + s.sum_x[2] + s.sum_x[3]).astype(BF16)

    def q_all(d):
        return push("q_all", d, s.qe.at[z], s.qe.at[z], at(next_z(d), y, x))

    start(NZ, q_all)
    loads[5].wait()
    arrive(2, l_own)
    arrive(NX, l_y)
    arrive(NZ, q_all)

    part = dot(s.qe[...].reshape(block, width), s.lp[...].reshape(d_z, width), COLS)
    s.t_part[...] = part.astype(BF16).reshape(NLAB, own, d_z)

    def t_sum(d):
        return push("t_sum", d, s.t_part.at[next_lab(d)], s.t_recv.at[y, j], {"lab": next_lab(d)})

    def t_cross(d):
        return push("t_cross", d, s.t_part.at[next_lab(d)], s.t_recv.at[y, j], across(d))

    start(NLAB, t_sum)
    start(NLAB + 1, t_cross)
    s.t_recv[y, j] = s.t_part[j]

    arrive(NLAB, count)
    counts = jnp.sum(s.c_recv[0] + s.c_recv[1] + s.c_recv[2] + s.c_recv[3], axis=0, keepdims=True)
    s.weight[...] = (1.0 - 0.99) / (1.0 - jnp.exp((counts + 1.0) * float(np.log(np.float64(np.float32(0.99))))))

    arrive(NLAB, t_sum)
    arrive(NLAB + 1, t_cross)
    mine = rows(z, d_z)
    total = s.t_recv[:, 0].astype(F32)
    for k in range(1, NLAB):
        total += s.t_recv[:, k].astype(F32)
    s.t[x, :, :, mine] = total.astype(BF16)

    def t_x(d):
        return push("t_x", d, s.t.at[x, 0, :, mine], s.t.at[x, 0, :, mine], at(z, y, next_x(d)))

    def t_z(d):
        return push("t_z", d, s.t.at[x, 1, :, mine], s.t.at[x, 1, :, mine], at(next_z(d), y, x))

    def t_xz(k):
        tile = s.t.at[lax.rem(x + NX - k, NX), 0, :, mine]
        return lambda d: push("t_xz", NZ * k + d, tile, tile, at(next_z(d), y, x))

    def t_zx(k):
        tile = s.t.at[x, 1, :, rows(lax.rem(z + NZ - k, NZ), d_z)]
        return lambda d: push("t_zx", NX * k + d, tile, tile, at(z, y, next_x(d)))

    def q_y(d):
        return push("q_y", d, s.qe, s.qe_peer, y_peer)

    start(NX, t_x)
    start(NZ, t_z)
    start(NZ, t_xz(0))
    start(NX, t_zx(0))
    for k in range(1, NX):
        t_x(k).wait_recv()
        start(NZ, t_xz(k))
        t_z(k).wait_recv()
        start(NX, t_zx(k))
    start(2, q_y)
    loads[6].wait()
    for k in range(NX):
        arrive(NZ, t_xz(k))
        arrive(NX, t_zx(k))

    def in_b(d):
        return lax.rem(z + lax.div(d, NY), NZ), lax.rem(y + lax.rem(d, NY), NY)

    def in_c(d):
        return lax.rem(x + lax.div(d, NY), NX), lax.rem(y + lax.rem(d, NY), NY)

    spot_b, spot_c = NY * z + y, NY * x + y

    def q_bx(d):
        nz, ny = in_b(d)
        return push("q_bx", d, s.qx_send.at[NY * nz + ny], s.qx.at[spot_b], at(nz, ny, x))

    def q_bz(d):
        nx, ny = in_c(d)
        return push("q_bz", d, s.qz_send.at[NY * nx + ny], s.qz.at[spot_c], at(z, ny, nx))

    start(NZ * NY, q_bx)
    start(NX * NY, q_bz)
    s.qx[spot_b] = s.qx_send[spot_b]
    s.qz[spot_c] = s.qz_send[spot_c]

    tall = 32

    def label_block(c, carry):
        cols = rows(c, wide)
        s.logit[...] = dot(s.t[...].reshape(here, wide_d), s.lh[cols, :], COLS) * temper
        weight = s.weight[:, cols]

        def row_block(r, loss):
            some = rows(r, tall)
            value = s.logit[some, :]
            hit = s.mask[some, cols] > 0.0
            value = jnp.where(hit, -value, value)
            small = jnp.exp(-jnp.abs(value))
            soft = jnp.maximum(value, 0.0) + jnp.log1p(small)
            over = 1.0 / (1.0 + small)
            under = small * over
            high = value >= 0.0
            chance, rest = jnp.where(high, over, under), jnp.where(high, under, over)
            square = chance * chance
            slope = weight * (square * (chance + 2.0 * rest * soft)) * temper
            s.gl[some, cols] = jnp.where(hit, -slope, slope).astype(BF16)
            return loss + jnp.sum((weight * (square * soft)).reshape(tall // 8, 8, wide), axis=0)

        s.l_part[:, cols] = lax.fori_loop(0, here // tall, row_block, jnp.zeros((8, wide), F32))
        return carry

    lax.fori_loop(0, n_label // wide, label_block, 0)

    def u_z(d):
        return push("u_z", d, s.u_part.at[:, 0, :, rows(next_z(d), d_z)], s.u_rz.at[z], at(next_z(d), y, x))

    def u_x(d):
        return push("u_x", d, s.u_part.at[next_x(d), 1], s.u_rx.at[x], at(z, y, next_x(d)))

    def u_zx(d):
        return push("u_zx", d, s.u_sz.at[next_x(d)], s.u_rzx.at[x], at(z, y, next_x(d)))

    def u_xz(d):
        return push("u_xz", d, s.u_sx.at[:, rows(next_z(d), d_z)], s.u_rxz.at[z], at(next_z(d), y, x))

    def u_block(d):
        cols = rows(next_z(d), d_z)
        part = dot(s.gl[...], s.lh[:, cols])
        s.u_part[:, :, :, cols] = part.astype(BF16).reshape(NX, NY, own, d_z)

    def u_turn(d):
        u_block(d)
        u_z(d).start()

    each(NZ, u_turn)
    sent.append((NZ, u_z))
    u_block(0)
    start(NX, u_x)

    def loss_sum(d):
        return push("loss", d, s.l_part, s.l_recv.at[j], {"lab": next_lab(d)})

    start(NLAB, loss_sum)
    s.l_recv[j] = s.l_part[...]
    arrive(NZ, u_z)
    half = s.u_part[:, 0, :, mine].astype(F32)
    for d in range(1, NZ):
        half += s.u_rz[next_z(d)].astype(F32)
    s.u_sz[...] = half.astype(BF16)
    start(NX, u_zx)
    arrive(NX, u_x)
    half = s.u_part[x, 1].astype(F32)
    for d in range(1, NX):
        half += s.u_rx[next_x(d)].astype(F32)
    s.u_sx[...] = half.astype(BF16)
    start(NZ, u_xz)
    arrive(NX, u_zx)
    half = s.u_sz[x].astype(F32)
    for d in range(1, NX):
        half += s.u_rzx[next_x(d)].astype(F32)
    s.back[0] = half
    arrive(NZ, u_xz)
    half = s.u_sx[:, mine].astype(F32)
    for d in range(1, NZ):
        half += s.u_rxz[next_z(d)].astype(F32)
    s.back[1] = half

    s.u_send[...] = s.back[...].astype(BF16)

    def u_all(d):
        return push("u_all", d, s.u_send.at[y], s.u.at[y, j], {"lab": next_lab(d)})

    def u_cross(d):
        return push("u_cross", d, s.u_send.at[1 - y], s.u.at[y, j], across(d))

    start(NLAB, u_all)
    start(NLAB + 1, u_cross)
    s.u[y, j] = s.u_send[y]
    arrive(NLAB, u_all)
    arrive(NLAB + 1, u_cross)
    u = [s.u[k].reshape(block, d_z) for k in range(NY)]

    s.u_sum[...] = (u[0].astype(F32) + u[1].astype(F32)).astype(BF16)

    def u_y(d):
        return push("u_y", d, s.u_sum, s.u_peer, y_peer)

    start(2, u_y)
    l_proj = s.lp[...].reshape(d_z, width)
    part = (dot(u[0], l_proj) + dot(u[1], l_proj)).reshape(NZ, own, width)
    s.g_part[...] = part
    s.g_send[...] = part.astype(BF16)

    def g_sum(d):
        return push("g_sum", d, s.g_send.at[next_z(d)], s.g_recv.at[z], at(next_z(d), y, x))

    start(NZ, g_sum)

    qe = s.qe[...].reshape(block, width)
    part = dot(u[0], qe, ROWS) + dot(u[1], qe, ROWS)
    arrive(2, q_y)
    arrive(2, u_y)
    part += dot(s.u_peer[...], s.qe_peer[...].reshape(block, width), ROWS)
    s.k_both[...] = part.reshape(NY, NX, d_row, width)
    s.k_send[...] = s.k_both[y].astype(BF16)

    def k_x(d):
        return push("k_x", d, s.k_send.at[next_x(d)], s.k_recv.at[x], at(z, y, next_x(d)))

    start(NX, k_x)
    arrive(NZ, g_sum)
    total = s.g_part[z]
    for d in range(1, NZ):
        total += s.g_recv[next_z(d)].astype(F32)
    gqe_out[...] = total
    s.ge[...] = total.astype(BF16)

    def g_yx(d):
        return push("g_yx", d, s.ge.at[:, x_cols], s.gx.at[spot_b], y_peer)

    def g_yz(d):
        return push("g_yz", d, s.ge.at[:, z_cols], s.gz.at[spot_c], y_peer)

    def g_z(d):
        return push("g_z", d, s.ge.at[:, x_cols], s.gx.at[spot_b], at(next_z(d), y, x))

    def g_x(d):
        return push("g_x", d, s.ge.at[:, z_cols], s.gz.at[spot_c], at(z, y, next_x(d)))

    def g_fz(d):
        other = s.gx.at[NY * z + 1 - y]
        return push("g_fz", d, other, other, at(next_z(d), y, x))

    def g_fx(d):
        other = s.gz.at[NY * x + 1 - y]
        return push("g_fx", d, other, other, at(z, y, next_x(d)))

    start(2, g_yx)
    start(2, g_yz)
    start(NZ, g_z)
    start(NX, g_x)
    arrive(2, g_yx)
    start(NZ, g_fz)
    arrive(2, g_yz)
    start(NX, g_fx)
    s.gx[spot_b] = s.ge[:, :cut]
    s.gz[spot_c] = s.ge[:, cut:]
    arrive(NLAB, loss_sum)
    losses = jnp.sum(s.l_recv[0] + s.l_recv[1] + s.l_recv[2] + s.l_recv[3], axis=0, keepdims=True)
    loss_out[...] = losses / (NQRY * own)
    arrive(NZ * NY, q_bx)
    arrive(NX * NY, q_bz)

    arrive(NZ, g_z)
    arrive(NZ, g_fz)
    part = dot(s.qx[...].reshape(here, e_b), s.gx[...].reshape(here, cut), ROWS).reshape(NX, e_row, cut)
    s.px_part[...] = part
    s.px_send[...] = part.astype(BF16)

    def p_x(d):
        return push("p_x", d, s.px_send.at[next_x(d)], s.px_recv.at[x], at(z, y, next_x(d)))

    start(NX, p_x)
    arrive(NX, g_x)
    arrive(NX, g_fx)
    part = dot(s.qz[...].reshape(here, e_b), s.gz[...].reshape(here, width - cut), ROWS).reshape(NZ, e_row, width - cut)
    s.pz_part[...] = part
    s.pz_send[...] = part.astype(BF16)

    def p_z(d):
        return push("p_z", d, s.pz_send.at[next_z(d)], s.pz_recv.at[z], at(next_z(d), y, x))

    start(NZ, p_z)

    arrive(NX, k_x)
    total = s.k_both[y, x]
    for d in range(1, NX):
        total += s.k_recv[next_x(d)].astype(F32)
    glp_out[...] = total
    arrive(NX, p_x)
    total = s.px_part[x]
    for d in range(1, NX):
        total += s.px_recv[next_x(d)].astype(F32)
    gqp_out[:, :cut] = total
    arrive(NZ, p_z)
    total = s.pz_part[z]
    for d in range(1, NZ):
        total += s.pz_recv[next_z(d)].astype(F32)
    gqp_out[:, cut:] = total

    for number, copies in sent:
        each(number, lambda d: copies(d).wait_send())
    ids_sent()


class Scratch:
    def __init__(self, names, refs):
        for name, ref in zip(names, refs):
            setattr(self, name, ref)


def shards(query_hidden, query_proj, label_hidden, label_proj, pos_ids, pos_count):
    own, wide_e = query_hidden.shape
    n_label, wide_d = label_hidden.shape
    e_row, width = query_proj.shape
    d_row = label_proj.shape[0]
    slots = pos_ids.shape[1]
    e_z, d_z, e_b = NX * NY * e_row, NX * NY * d_row, NX * e_row
    here, block = NX * NY * own, NZ * own
    cut = width // 256 * 128
    rest = width - cut
    scratch = {
        "qh": ((own, wide_e), BF16),
        "ids_raw": ((slots, own), jnp.int32),
        "used": ((1, own), jnp.int32),
        "ids_send": ((slots, 128), jnp.int32),
        "ids": ((NX, NY, slots, 128), jnp.int32),
        "lh": ((n_label, wide_d), BF16),
        "lp": ((NY, NX, d_row, width), BF16),
        "wx": ((NY, NX, e_row, cut), BF16),
        "wz": ((NZ, NY, e_row, rest), BF16),
        "q0": ((NZ, own, e_z), BF16),
        "q1_send": ((NX, own, e_z), BF16),
        "q1": ((NX, own, e_z), BF16),
        "qx_send": ((NZ * NY, own, e_b), BF16),
        "qx": ((NZ * NY, own, e_b), BF16),
        "qz_send": ((NX * NY, own, e_b), BF16),
        "qz": ((NX * NY, own, e_b), BF16),
        "part_z": ((NZ, own, cut), F32),
        "sum_z": ((NZ, own, cut), F32),
        "part_x": ((NX, own, rest), F32),
        "sum_x": ((NX, own, rest), F32),
        "mask": ((here, n_label), F32),
        "c_part": ((8, n_label), F32),
        "c_recv": ((NLAB, 8, n_label), F32),
        "weight": ((1, n_label), F32),
        "qe": ((NZ, own, width), BF16),
        "t_part": ((NLAB, own, d_z), BF16),
        "t_recv": ((NY, NLAB, own, d_z), BF16),
        "t": ((NX, NY, own, wide_d), BF16),
        "logit": ((here, 256), F32),
        "gl": ((here, n_label), BF16),
        "l_part": ((8, n_label), F32),
        "l_recv": ((NLAB, 8, n_label), F32),
        "u_part": ((NX, NY, own, wide_d), BF16),
        "u_rz": ((NZ, NX, own, d_z), BF16),
        "u_rx": ((NX, own, wide_d), BF16),
        "u_sz": ((NX, own, d_z), BF16),
        "u_sx": ((own, wide_d), BF16),
        "u_rzx": ((NX, own, d_z), BF16),
        "u_rxz": ((NZ, own, d_z), BF16),
        "back": ((NY, own, d_z), F32),
        "u_send": ((NY, own, d_z), BF16),
        "u": ((NY, NLAB, own, d_z), BF16),
        "u_sum": ((block, d_z), BF16),
        "u_peer": ((block, d_z), BF16),
        "qe_peer": ((NZ, own, width), BF16),
        "g_part": ((NZ, own, width), F32),
        "g_send": ((NZ, own, width), BF16),
        "g_recv": ((NZ, own, width), BF16),
        "ge": ((own, width), BF16),
        "gx": ((NZ * NY, own, cut), BF16),
        "gz": ((NX * NY, own, rest), BF16),
        "k_both": ((NY, NX, d_row, width), F32),
        "k_send": ((NX, d_row, width), BF16),
        "k_recv": ((NX, d_row, width), BF16),
        "px_part": ((NX, e_row, cut), F32),
        "px_send": ((NX, e_row, cut), BF16),
        "px_recv": ((NX, e_row, cut), BF16),
        "pz_part": ((NZ, e_row, rest), F32),
        "pz_send": ((NZ, e_row, rest), BF16),
        "pz_recv": ((NZ, e_row, rest), BF16),
    }
    scratch = {name: pltpu.VMEM(*spec) for name, spec in scratch.items()}
    scratch["load"] = pltpu.SemaphoreType.DMA((7,))
    pairs = ("w_yx", "w_yz", "l_own", "i_y", "g_yx", "g_yz", "q_y", "u_y")
    fours = (
        "w_x", "w_z", "w_fx", "w_fz", "q0", "q1", "l_x", "l_y", "i_x", "i_z", "b_z", "b_x", "count", "q_all", "t_sum",
        "t_x", "t_z", "u_z", "u_x", "u_zx", "u_xz", "loss", "u_all", "g_sum", "g_z", "g_x", "g_fz", "g_fx", "k_x", "p_x", "p_z",
    )
    fives, eights = ("t_cross", "u_cross"), ("q_bx", "q_bz")
    sixteens = ("t_xz", "t_zx")
    for number, group in ((2, pairs), (4, fours), (5, fives), (8, eights), (16, sixteens)):
        for name in group:
            scratch["send_" + name] = pltpu.SemaphoreType.DMA((number,))
            scratch["recv_" + name] = pltpu.SemaphoreType.DMA((number,))
    names = tuple(scratch)

    def kernel(*refs):
        step_kernel(wide_e ** (-0.5), cut, *refs[:10], Scratch(names, refs[10:]))

    arrays = [
        pltpu.with_memory_space_constraint(a, pltpu.HBM)
        for a in (query_hidden, query_proj, label_hidden, label_proj, pos_ids.T, pos_count.reshape(1, own))
    ]
    gqp, glp, loss, gqe = pl.pallas_call(
        kernel,
        out_shape=(
            jax.ShapeDtypeStruct((e_row, width), F32),
            jax.ShapeDtypeStruct((d_row, width), F32),
            jax.ShapeDtypeStruct((1, n_label), F32),
            jax.ShapeDtypeStruct((own, width), F32),
        ),
        in_specs=[pl.BlockSpec(memory_space=pltpu.HBM)] * 6,
        out_specs=(pl.BlockSpec(memory_space=pltpu.VMEM),) * 4,
        scratch_shapes=list(scratch.values()),
        compiler_params=pltpu.CompilerParams(
            collective_id=0, has_side_effects=True, vmem_limit_bytes=48 << 20
        ),
        name="focal_step",
    )(*arrays)
    return gqp, glp, loss.reshape(n_label), gqe


def solution(mesh):
    in_specs = (
        P("qry", None),
        P("qry", "lab"),
        P("qry", None),
        P("qry", "lab"),
        P("qry", None),
        P("qry"),
    )
    out_specs = (P("qry", "lab"), P("qry", "lab"), P("qry"), P("qry", "lab"))
    return jax.shard_map(shards, mesh=mesh, in_specs=in_specs, out_specs=out_specs, check_vma=False)
```

```python
import jax
import jax.numpy as jnp
import numpy as np
from jax import lax
from jax.experimental import pallas as pl
from jax.experimental.pallas import tpu as pltpu
from jax.sharding import PartitionSpec as P

NX, NY, NZ, NLAB = 4, 2, 4, 4
NQRY = NX * NY * NZ
ROWS = (((0,), (0,)), ((), ()))
COLS = (((1,), (1,)), ((), ()))
MESH = pl.DeviceIdType.MESH
F32, BF16 = jnp.float32, jnp.bfloat16


def dot(left, right, dims=(((1,), (0,)), ((), ()))):
    return lax.dot_general(left, right, dims, preferred_element_type=F32)


def each(count, step):
    for d in range(1, count):
        step(d)


def step_kernel(temper, cut, qh, qp, lh, lp, ids, used, gqp_out, glp_out, loss_out, gqe_out, s):
    own = qh.shape[0]
    e_row, d_row, width = qp.shape[0], lp.shape[0], qp.shape[1]
    n_label, wide_d = lh.shape
    e_z, d_z = NX * NY * e_row, NX * NY * d_row
    e_b = NX * e_row
    here, block = NX * NY * own, NZ * own
    me, j = lax.axis_index("qry"), lax.axis_index("lab")
    x, y, z = lax.rem(me, NX), lax.rem(lax.div(me, NX), NY), lax.div(me, NX * NY)

    def at(nz, ny, nx):
        return {"qry": (nz * NY + ny) * NX + nx}

    y_peer = at(z, 1 - y, x)

    def next_x(d):
        return lax.rem(x + d, NX)

    def next_z(d):
        return lax.rem(z + d, NZ)

    def next_lab(d):
        return lax.rem(j + d, NLAB)

    def across(d):
        return {**y_peer, "lab": next_lab(d)}

    def rows(index, size):
        return pl.ds(pl.multiple_of(index * size, size), size)

    def push(name, d, src, dst, device):
        return pltpu.make_async_remote_copy(
            src_ref=src,
            dst_ref=dst,
            send_sem=getattr(s, "send_" + name).at[d],
            recv_sem=getattr(s, "recv_" + name).at[d],
            device_id=device,
            device_id_type=MESH,
        )

    sent = []

    def start(count, copies):
        each(count, lambda d: copies(d).start())
        sent.append((count, copies))

    def arrive(count, copies):
        each(count, lambda d: copies(d).wait_recv())

    loads = [
        pltpu.make_async_copy(source, target, s.load.at[k])
        for k, (source, target) in enumerate(
            (
                (qh, s.qh),
                (ids, s.ids_raw),
                (used, s.used),
                (qp.at[:, pl.ds(0, cut)], s.wx.at[y, x]),
                (qp.at[:, pl.ds(cut, width - cut)], s.wz.at[z, y]),
                (lp, s.lp.at[y, x]),
                (lh, s.lh),
            )
        )
    ]
    for load in loads:
        load.start()

    barrier = pltpu.get_barrier_semaphore()

    def greet(device):
        pl.semaphore_signal(barrier, inc=1, device_id=device, device_id_type=MESH)

    each(NX, lambda d: greet(at(z, y, next_x(d))))
    each(NZ, lambda d: greet(at(next_z(d), y, x)))
    greet(y_peer)
    each(NX, lambda d: greet(at(z, 1 - y, next_x(d))))
    each(NZ, lambda d: greet(at(next_z(d), 1 - y, x)))
    each(NLAB, lambda d: greet({"lab": next_lab(d)}))
    each(NLAB, lambda d: greet(across(d)))

    loads[0].wait()
    for k in range(NX):
        s.q1_send[k] = jnp.concatenate(
            [s.qh[:, (NX * r + k) * e_row : (NX * r + k + 1) * e_row] for r in range(NZ * NY)], axis=1
        )
    for k in range(NZ * NY):
        s.qx_send[k] = s.qh[:, k * e_b : (k + 1) * e_b]
    for nx in range(NX):
        for ny in range(NY):
            first = [(NX * (NY * r + ny) + nx) * e_row for r in range(NZ)]
            s.qz_send[NY * nx + ny] = jnp.concatenate([s.qh[:, f : f + e_row] for f in first], axis=1)
    loads[1].wait()
    loads[2].wait()
    slots = ids.shape[0]
    s.ids_send[...] = jnp.full(s.ids_send.shape, -1, jnp.int32)
    slot_at = lax.broadcasted_iota(jnp.int32, ids.shape, 0)
    s.ids_send[:, :own] = jnp.where(slot_at < s.used[...], s.ids_raw[...], -1)
    pl.semaphore_wait(barrier, 2 * (NX - 1) + 2 * (NZ - 1) + 1 + 2 * (NLAB - 1))

    x_cols, z_cols = pl.ds(0, cut), pl.ds(cut, width - cut)

    def w_yx(d):
        return push("w_yx", d, qp.at[:, x_cols], s.wx.at[y, x], y_peer)

    def w_yz(d):
        return push("w_yz", d, qp.at[:, z_cols], s.wz.at[z, y], y_peer)

    def w_x(d):
        return push("w_x", d, qp.at[:, x_cols], s.wx.at[y, x], at(z, y, next_x(d)))

    def w_z(d):
        return push("w_z", d, qp.at[:, z_cols], s.wz.at[z, y], at(next_z(d), y, x))

    def w_fx(d):
        return push("w_fx", d, s.wx.at[1 - y, x], s.wx.at[1 - y, x], at(z, y, next_x(d)))

    def w_fz(d):
        return push("w_fz", d, s.wz.at[z, 1 - y], s.wz.at[z, 1 - y], at(next_z(d), y, x))

    def q0(d):
        return push("q0", d, qh.at[:, rows(next_z(d), e_z)], s.q0.at[z], at(next_z(d), y, x))

    def q1(d):
        return push("q1", d, s.q1_send.at[next_x(d)], s.q1.at[x], at(z, y, next_x(d)))

    def l_x(d):
        return push("l_x", d, lp, s.lp.at[y, x], at(z, y, next_x(d)))

    def l_own(d):
        return push("l_own", d, lp, s.lp.at[y, x], y_peer)

    def l_y(d):
        block_at = s.lp.at[y, lax.rem(x + NX - d, NX)]
        return push("l_y", d, block_at, block_at, y_peer)

    start(NX, l_x)
    start(2, w_yx)
    start(2, w_yz)
    start(2, l_own)
    start(NX, w_x)
    start(NZ, w_z)
    start(NZ, q0)
    start(NX, q1)

    def i_y(d):
        return push("i_y", d, s.ids_send, s.ids.at[x, y], y_peer)

    def i_x(d):
        return push("i_x", d, s.ids.at[x], s.ids.at[x], at(z, y, next_x(d)))

    def i_z(d):
        return push("i_z", d, s.ids, s.ids, at(next_z(d), y, x))

    holder = z == j

    @pl.when(holder)
    def _():
        i_y(1).start()
        s.ids[x, y] = s.ids_send[...]
        i_y(1).wait_recv()
        each(NX, lambda d: i_x(d).start())

    s.q0[z] = s.qh[:, rows(z, e_z)]
    s.q1[x] = s.q1_send[x]
    arrive(2, w_yx)
    start(NX, w_fx)
    arrive(2, w_yz)
    start(NZ, w_fz)

    @pl.when(holder)
    def _():
        arrive(NX, i_x)
        each(NZ, lambda d: i_z(d).start())

    def ids_arrive():
        @pl.when(jnp.logical_not(holder))
        def _():
            i_z(lax.rem(z - j + NZ, NZ)).wait_recv()

    def ids_sent():
        @pl.when(holder)
        def _():
            i_y(1).wait_send()
            each(NX, lambda d: i_x(d).wait_send())
            each(NZ, lambda d: i_z(d).wait_send())

    arrive(NX, l_x)
    start(NX, l_y)

    arrive(NZ, q0)
    arrive(NX, w_x)
    loads[3].wait()
    arrive(NX, w_fx)
    s.part_z[...] = dot(s.q0[...].reshape(block, e_z), s.wx[...].reshape(e_z, cut)).reshape(NZ, own, cut)

    def b_z(d):
        return push("b_z", d, s.part_z.at[next_z(d)], s.sum_z.at[z], at(next_z(d), y, x))

    start(NZ, b_z)
    arrive(NX, q1)
    arrive(NZ, w_z)
    loads[4].wait()
    arrive(NZ, w_fz)
    s.part_x[...] = dot(s.q1[...].reshape(block, e_z), s.wz[...].reshape(e_z, width - cut)).reshape(NX, own, width - cut)

    def b_x(d):
        return push("b_x", d, s.part_x.at[next_x(d)], s.sum_x.at[x], at(z, y, next_x(d)))

    start(NX, b_x)
    s.sum_z[z] = s.part_z[z]
    s.sum_x[x] = s.part_x[x]

    ids_arrive()
    local = s.ids[...].reshape(NX * NY * slots, s.ids.shape[3]).T - n_label * me
    wide = 256
    for c in range(n_label // wide):
        column = lax.broadcasted_iota(jnp.int32, (own, wide), 1) + c * wide
        tally = jnp.zeros((8, wide), F32)
        for k in range(NX * NY):
            found = jnp.zeros((own, wide), F32)
            for slot in range(k * slots, (k + 1) * slots):
                found += jnp.where(local[:own, slot : slot + 1] == column, 1.0, 0.0)
            s.mask[k * own : (k + 1) * own, c * wide : (c + 1) * wide] = found
            tally += jnp.sum(found.reshape(own // 8, 8, wide), axis=0)
        s.c_part[:, c * wide : (c + 1) * wide] = tally

    def count(d):
        return push("count", d, s.c_part, s.c_recv.at[j], {"lab": next_lab(d)})

    start(NLAB, count)
    s.c_recv[j] = s.c_part[...]

    arrive(NZ, b_z)
    s.qe[z, :, :cut] = (s.sum_z[0] + s.sum_z[1] + s.sum_z[2] + s.sum_z[3]).astype(BF16)
    arrive(NX, b_x)
    s.qe[z, :, cut:] = (s.sum_x[0] + s.sum_x[1] + s.sum_x[2] + s.sum_x[3]).astype(BF16)

    def q_all(d):
        return push("q_all", d, s.qe.at[z], s.qe.at[z], at(next_z(d), y, x))

    start(NZ, q_all)
    loads[5].wait()
    arrive(2, l_own)
    arrive(NX, l_y)
    arrive(NZ, q_all)

    part = dot(s.qe[...].reshape(block, width), s.lp[...].reshape(d_z, width), COLS)
    s.t_part[...] = part.astype(BF16).reshape(NLAB, own, d_z)

    def t_sum(d):
        return push("t_sum", d, s.t_part.at[next_lab(d)], s.t_recv.at[y, j], {"lab": next_lab(d)})

    def t_cross(d):
        return push("t_cross", d, s.t_part.at[next_lab(d)], s.t_recv.at[y, j], across(d))

    start(NLAB, t_sum)
    start(NLAB + 1, t_cross)
    s.t_recv[y, j] = s.t_part[j]

    arrive(NLAB, count)
    counts = jnp.sum(s.c_recv[0] + s.c_recv[1] + s.c_recv[2] + s.c_recv[3], axis=0, keepdims=True)
    s.weight[...] = (1.0 - 0.99) / (1.0 - jnp.exp((counts + 1.0) * float(np.log(np.float64(np.float32(0.99))))))

    arrive(NLAB, t_sum)
    arrive(NLAB + 1, t_cross)
    mine = rows(z, d_z)
    total = s.t_recv[:, 0].astype(F32)
    for k in range(1, NLAB):
        total += s.t_recv[:, k].astype(F32)
    s.t[x, :, :, mine] = total.astype(BF16)

    def t_x(d):
        return push("t_x", d, s.t.at[x, 0, :, mine], s.t.at[x, 0, :, mine], at(z, y, next_x(d)))

    def t_z(d):
        return push("t_z", d, s.t.at[x, 1, :, mine], s.t.at[x, 1, :, mine], at(next_z(d), y, x))

    def t_xz(k):
        tile = s.t.at[lax.rem(x + NX - k, NX), 0, :, mine]
        return lambda d: push("t_xz", NZ * k + d, tile, tile, at(next_z(d), y, x))

    def t_zx(k):
        tile = s.t.at[x, 1, :, rows(lax.rem(z + NZ - k, NZ), d_z)]
        return lambda d: push("t_zx", NX * k + d, tile, tile, at(z, y, next_x(d)))

    def q_y(d):
        return push("q_y", d, s.qe, s.qe_peer, y_peer)

    start(NX, t_x)
    start(NZ, t_z)
    start(NZ, t_xz(0))
    start(NX, t_zx(0))
    for k in range(1, NX):
        t_x(k).wait_recv()
        start(NZ, t_xz(k))
        t_z(k).wait_recv()
        start(NX, t_zx(k))
    loads[6].wait()
    for k in range(NX):
        arrive(NZ, t_xz(k))
        arrive(NX, t_zx(k))

    def in_b(d):
        return lax.rem(z + lax.div(d, NY), NZ), lax.rem(y + lax.rem(d, NY), NY)

    def in_c(d):
        return lax.rem(x + lax.div(d, NY), NX), lax.rem(y + lax.rem(d, NY), NY)

    spot_b, spot_c = NY * z + y, NY * x + y

    def q_bx(d):
        nz, ny = in_b(d)
        return push("q_bx", d, s.qx_send.at[NY * nz + ny], s.qx.at[spot_b], at(nz, ny, x))

    def q_bz(d):
        nx, ny = in_c(d)
        return push("q_bz", d, s.qz_send.at[NY * nx + ny], s.qz.at[spot_c], at(z, ny, nx))

    start(NZ * NY, q_bx)
    start(NX * NY, q_bz)
    s.qx[spot_b] = s.qx_send[spot_b]
    s.qz[spot_c] = s.qz_send[spot_c]

    start(2, q_y)
    tall = 32

    def label_block(c, carry):
        cols = rows(c, wide)
        s.logit[...] = dot(s.t[...].reshape(here, wide_d), s.lh[cols, :], COLS) * temper
        weight = s.weight[:, cols]

        def row_block(r, loss):
            some = rows(r, tall)
            value = s.logit[some, :]
            hit = s.mask[some, cols] > 0.0
            value = jnp.where(hit, -value, value)
            small = jnp.exp(-jnp.abs(value))
            soft = jnp.maximum(value, 0.0) + jnp.log1p(small)
            over = 1.0 / (1.0 + small)
            under = small * over
            high = value >= 0.0
            chance, rest = jnp.where(high, over, under), jnp.where(high, under, over)
            square = chance * chance
            slope = weight * (square * (chance + 2.0 * rest * soft)) * temper
            s.gl[some, cols] = jnp.where(hit, -slope, slope).astype(BF16)
            return loss + jnp.sum((weight * (square * soft)).reshape(tall // 8, 8, wide), axis=0)

        s.l_part[:, cols] = lax.fori_loop(0, here // tall, row_block, jnp.zeros((8, wide), F32), unroll=True)
        return carry

    lax.fori_loop(0, n_label // wide, label_block, 0)

    def u_z(d):
        return push("u_z", d, s.u_part.at[:, 0, :, rows(next_z(d), d_z)], s.u_rz.at[z], at(next_z(d), y, x))

    def u_x(d):
        return push("u_x", d, s.u_part.at[next_x(d), 1], s.u_rx.at[x], at(z, y, next_x(d)))

    def u_zx(d):
        return push("u_zx", d, s.u_sz.at[next_x(d)], s.u_rzx.at[x], at(z, y, next_x(d)))

    def u_xz(d):
        return push("u_xz", d, s.u_sx.at[:, rows(next_z(d), d_z)], s.u_rxz.at[z], at(next_z(d), y, x))

    def u_block(d):
        cols = rows(next_z(d), d_z)
        part = dot(s.gl[...], s.lh[:, cols])
        s.u_part[:, :, :, cols] = part.astype(BF16).reshape(NX, NY, own, d_z)

    def u_turn(d):
        u_block(d)
        u_z(d).start()

    each(NZ, u_turn)
    sent.append((NZ, u_z))
    u_block(0)
    start(NX, u_x)

    def loss_sum(d):
        return push("loss", d, s.l_part, s.l_recv.at[j], {"lab": next_lab(d)})

    start(NLAB, loss_sum)
    s.l_recv[j] = s.l_part[...]
    arrive(NZ, u_z)
    half = s.u_part[:, 0, :, mine].astype(F32)
    for d in range(1, NZ):
        half += s.u_rz[next_z(d)].astype(F32)
    s.u_sz[...] = half.astype(BF16)
    start(NX, u_zx)
    arrive(NX, u_x)
    half = s.u_part[x, 1].astype(F32)
    for d in range(1, NX):
        half += s.u_rx[next_x(d)].astype(F32)
    s.u_sx[...] = half.astype(BF16)
    start(NZ, u_xz)
    arrive(NX, u_zx)
    half = s.u_sz[x].astype(F32)
    for d in range(1, NX):
        half += s.u_rzx[next_x(d)].astype(F32)
    s.back[0] = half
    arrive(NZ, u_xz)
    half = s.u_sx[:, mine].astype(F32)
    for d in range(1, NZ):
        half += s.u_rxz[next_z(d)].astype(F32)
    s.back[1] = half

    s.u_send[...] = s.back[...].astype(BF16)

    def u_all(d):
        return push("u_all", d, s.u_send.at[y], s.u.at[y, j], {"lab": next_lab(d)})

    def u_cross(d):
        return push("u_cross", d, s.u_send.at[1 - y], s.u.at[y, j], across(d))

    start(NLAB, u_all)
    start(NLAB + 1, u_cross)
    s.u[y, j] = s.u_send[y]
    arrive(NLAB, u_all)
    arrive(NLAB + 1, u_cross)
    u = [s.u[k].reshape(block, d_z) for k in range(NY)]

    s.u_sum[...] = (u[0].astype(F32) + u[1].astype(F32)).astype(BF16)

    def u_y(d):
        return push("u_y", d, s.u_sum, s.u_peer, y_peer)

    start(2, u_y)
    l_proj = s.lp[...].reshape(d_z, width)
    part = (dot(u[0], l_proj) + dot(u[1], l_proj)).reshape(NZ, own, width)
    s.g_part[...] = part
    s.g_send[...] = part.astype(BF16)

    def g_sum(d):
        return push("g_sum", d, s.g_send.at[next_z(d)], s.g_recv.at[z], at(next_z(d), y, x))

    start(NZ, g_sum)

    qe = s.qe[...].reshape(block, width)
    part = dot(u[0], qe, ROWS) + dot(u[1], qe, ROWS)
    arrive(2, q_y)
    arrive(2, u_y)
    part += dot(s.u_peer[...], s.qe_peer[...].reshape(block, width), ROWS)
    s.k_both[...] = part.reshape(NY, NX, d_row, width)
    s.k_send[...] = s.k_both[y].astype(BF16)

    def k_x(d):
        return push("k_x", d, s.k_send.at[next_x(d)], s.k_recv.at[x], at(z, y, next_x(d)))

    start(NX, k_x)
    arrive(NZ, g_sum)
    total = s.g_part[z]
    for d in range(1, NZ):
        total += s.g_recv[next_z(d)].astype(F32)
    gqe_out[...] = total
    s.ge[...] = total.astype(BF16)

    def g_yx(d):
        return push("g_yx", d, s.ge.at[:, x_cols], s.gx.at[spot_b], y_peer)

    def g_yz(d):
        return push("g_yz", d, s.ge.at[:, z_cols], s.gz.at[spot_c], y_peer)

    def g_z(d):
        return push("g_z", d, s.ge.at[:, x_cols], s.gx.at[spot_b], at(next_z(d), y, x))

    def g_x(d):
        return push("g_x", d, s.ge.at[:, z_cols], s.gz.at[spot_c], at(z, y, next_x(d)))

    def g_fz(d):
        other = s.gx.at[NY * z + 1 - y]
        return push("g_fz", d, other, other, at(next_z(d), y, x))

    def g_fx(d):
        other = s.gz.at[NY * x + 1 - y]
        return push("g_fx", d, other, other, at(z, y, next_x(d)))

    start(2, g_yx)
    start(2, g_yz)
    start(NZ, g_z)
    start(NX, g_x)
    arrive(2, g_yx)
    start(NZ, g_fz)
    arrive(2, g_yz)
    start(NX, g_fx)
    s.gx[spot_b] = s.ge[:, :cut]
    s.gz[spot_c] = s.ge[:, cut:]
    arrive(NLAB, loss_sum)
    losses = jnp.sum(s.l_recv[0] + s.l_recv[1] + s.l_recv[2] + s.l_recv[3], axis=0, keepdims=True)
    loss_out[...] = losses / (NQRY * own)
    arrive(NZ * NY, q_bx)
    arrive(NX * NY, q_bz)

    arrive(NZ, g_z)
    arrive(NZ, g_fz)
    part = dot(s.qx[...].reshape(here, e_b), s.gx[...].reshape(here, cut), ROWS).reshape(NX, e_row, cut)
    s.px_part[...] = part
    s.px_send[...] = part.astype(BF16)

    def p_x(d):
        return push("p_x", d, s.px_send.at[next_x(d)], s.px_recv.at[x], at(z, y, next_x(d)))

    start(NX, p_x)
    arrive(NX, g_x)
    arrive(NX, g_fx)
    part = dot(s.qz[...].reshape(here, e_b), s.gz[...].reshape(here, width - cut), ROWS).reshape(NZ, e_row, width - cut)
    s.pz_part[...] = part
    s.pz_send[...] = part.astype(BF16)

    def p_z(d):
        return push("p_z", d, s.pz_send.at[next_z(d)], s.pz_recv.at[z], at(next_z(d), y, x))

    start(NZ, p_z)

    arrive(NX, k_x)
    total = s.k_both[y, x]
    for d in range(1, NX):
        total += s.k_recv[next_x(d)].astype(F32)
    glp_out[...] = total
    arrive(NX, p_x)
    total = s.px_part[x]
    for d in range(1, NX):
        total += s.px_recv[next_x(d)].astype(F32)
    gqp_out[:, :cut] = total
    arrive(NZ, p_z)
    total = s.pz_part[z]
    for d in range(1, NZ):
        total += s.pz_recv[next_z(d)].astype(F32)
    gqp_out[:, cut:] = total

    for number, copies in sent:
        each(number, lambda d: copies(d).wait_send())
    ids_sent()


class Scratch:
    def __init__(self, names, refs):
        for name, ref in zip(names, refs):
            setattr(self, name, ref)


def shards(query_hidden, query_proj, label_hidden, label_proj, pos_ids, pos_count):
    own, wide_e = query_hidden.shape
    n_label, wide_d = label_hidden.shape
    e_row, width = query_proj.shape
    d_row = label_proj.shape[0]
    slots = pos_ids.shape[1]
    e_z, d_z, e_b = NX * NY * e_row, NX * NY * d_row, NX * e_row
    here, block = NX * NY * own, NZ * own
    cut = width // 256 * 128
    rest = width - cut
    scratch = {
        "qh": ((own, wide_e), BF16),
        "ids_raw": ((slots, own), jnp.int32),
        "used": ((1, own), jnp.int32),
        "ids_send": ((slots, 128), jnp.int32),
        "ids": ((NX, NY, slots, 128), jnp.int32),
        "lh": ((n_label, wide_d), BF16),
        "lp": ((NY, NX, d_row, width), BF16),
        "wx": ((NY, NX, e_row, cut), BF16),
        "wz": ((NZ, NY, e_row, rest), BF16),
        "q0": ((NZ, own, e_z), BF16),
        "q1_send": ((NX, own, e_z), BF16),
        "q1": ((NX, own, e_z), BF16),
        "qx_send": ((NZ * NY, own, e_b), BF16),
        "qx": ((NZ * NY, own, e_b), BF16),
        "qz_send": ((NX * NY, own, e_b), BF16),
        "qz": ((NX * NY, own, e_b), BF16),
        "part_z": ((NZ, own, cut), F32),
        "sum_z": ((NZ, own, cut), F32),
        "part_x": ((NX, own, rest), F32),
        "sum_x": ((NX, own, rest), F32),
        "mask": ((here, n_label), F32),
        "c_part": ((8, n_label), F32),
        "c_recv": ((NLAB, 8, n_label), F32),
        "weight": ((1, n_label), F32),
        "qe": ((NZ, own, width), BF16),
        "t_part": ((NLAB, own, d_z), BF16),
        "t_recv": ((NY, NLAB, own, d_z), BF16),
        "t": ((NX, NY, own, wide_d), BF16),
        "logit": ((here, 256), F32),
        "gl": ((here, n_label), BF16),
        "l_part": ((8, n_label), F32),
        "l_recv": ((NLAB, 8, n_label), F32),
        "u_part": ((NX, NY, own, wide_d), BF16),
        "u_rz": ((NZ, NX, own, d_z), BF16),
        "u_rx": ((NX, own, wide_d), BF16),
        "u_sz": ((NX, own, d_z), BF16),
        "u_sx": ((own, wide_d), BF16),
        "u_rzx": ((NX, own, d_z), BF16),
        "u_rxz": ((NZ, own, d_z), BF16),
        "back": ((NY, own, d_z), F32),
        "u_send": ((NY, own, d_z), BF16),
        "u": ((NY, NLAB, own, d_z), BF16),
        "u_sum": ((block, d_z), BF16),
        "u_peer": ((block, d_z), BF16),
        "qe_peer": ((NZ, own, width), BF16),
        "g_part": ((NZ, own, width), F32),
        "g_send": ((NZ, own, width), BF16),
        "g_recv": ((NZ, own, width), BF16),
        "ge": ((own, width), BF16),
        "gx": ((NZ * NY, own, cut), BF16),
        "gz": ((NX * NY, own, rest), BF16),
        "k_both": ((NY, NX, d_row, width), F32),
        "k_send": ((NX, d_row, width), BF16),
        "k_recv": ((NX, d_row, width), BF16),
        "px_part": ((NX, e_row, cut), F32),
        "px_send": ((NX, e_row, cut), BF16),
        "px_recv": ((NX, e_row, cut), BF16),
        "pz_part": ((NZ, e_row, rest), F32),
        "pz_send": ((NZ, e_row, rest), BF16),
        "pz_recv": ((NZ, e_row, rest), BF16),
    }
    scratch = {name: pltpu.VMEM(*spec) for name, spec in scratch.items()}
    scratch["load"] = pltpu.SemaphoreType.DMA((7,))
    pairs = ("w_yx", "w_yz", "l_own", "i_y", "g_yx", "g_yz", "q_y", "u_y")
    fours = (
        "w_x", "w_z", "w_fx", "w_fz", "q0", "q1", "l_x", "l_y", "i_x", "i_z", "b_z", "b_x", "count", "q_all", "t_sum",
        "t_x", "t_z", "u_z", "u_x", "u_zx", "u_xz", "loss", "u_all", "g_sum", "g_z", "g_x", "g_fz", "g_fx", "k_x", "p_x", "p_z",
    )
    fives, eights = ("t_cross", "u_cross"), ("q_bx", "q_bz")
    sixteens = ("t_xz", "t_zx")
    for number, group in ((2, pairs), (4, fours), (5, fives), (8, eights), (16, sixteens)):
        for name in group:
            scratch["send_" + name] = pltpu.SemaphoreType.DMA((number,))
            scratch["recv_" + name] = pltpu.SemaphoreType.DMA((number,))
    names = tuple(scratch)

    def kernel(*refs):
        step_kernel(wide_e ** (-0.5), cut, *refs[:10], Scratch(names, refs[10:]))

    arrays = [
        pltpu.with_memory_space_constraint(a, pltpu.HBM)
        for a in (query_hidden, query_proj, label_hidden, label_proj, pos_ids.T, pos_count.reshape(1, own))
    ]
    gqp, glp, loss, gqe = pl.pallas_call(
        kernel,
        out_shape=(
            jax.ShapeDtypeStruct((e_row, width), F32),
            jax.ShapeDtypeStruct((d_row, width), F32),
            jax.ShapeDtypeStruct((1, n_label), F32),
            jax.ShapeDtypeStruct((own, width), F32),
        ),
        in_specs=[pl.BlockSpec(memory_space=pltpu.HBM)] * 6,
        out_specs=(pl.BlockSpec(memory_space=pltpu.VMEM),) * 4,
        scratch_shapes=list(scratch.values()),
        compiler_params=pltpu.CompilerParams(
            collective_id=0, has_side_effects=True, vmem_limit_bytes=48 << 20
        ),
        name="focal_step",
    )(*arrays)
    return gqp, glp, loss.reshape(n_label), gqe


def solution(mesh):
    in_specs = (
        P("qry", None),
        P("qry", "lab"),
        P("qry", None),
        P("qry", "lab"),
        P("qry", None),
        P("qry"),
    )
    out_specs = (P("qry", "lab"), P("qry", "lab"), P("qry"), P("qry", "lab"))
    return jax.shard_map(shards, mesh=mesh, in_specs=in_specs, out_specs=out_specs, check_vma=False)
```

```python
import jax
import jax.numpy as jnp
import numpy as np
from jax import lax
from jax.experimental import pallas as pl
from jax.experimental.pallas import tpu as pltpu
from jax.sharding import PartitionSpec as P

NX, NY, NZ, NLAB = 4, 2, 4, 4
NQRY = NX * NY * NZ
ROWS = (((0,), (0,)), ((), ()))
COLS = (((1,), (1,)), ((), ()))
MESH = pl.DeviceIdType.MESH
F32, BF16 = jnp.float32, jnp.bfloat16


def dot(left, right, dims=(((1,), (0,)), ((), ()))):
    return lax.dot_general(left, right, dims, preferred_element_type=F32)


def each(count, step):
    for d in range(1, count):
        step(d)


def step_kernel(temper, cut, qh, qp, lh, lp, ids, used, gqp_out, glp_out, loss_out, gqe_out, s):
    own = qh.shape[0]
    e_row, d_row, width = qp.shape[0], lp.shape[0], qp.shape[1]
    n_label, wide_d = lh.shape
    e_z, d_z = NX * NY * e_row, NX * NY * d_row
    e_b = NX * e_row
    here, block = NX * NY * own, NZ * own
    me, j = lax.axis_index("qry"), lax.axis_index("lab")
    x, y, z = lax.rem(me, NX), lax.rem(lax.div(me, NX), NY), lax.div(me, NX * NY)

    def at(nz, ny, nx):
        return {"qry": (nz * NY + ny) * NX + nx}

    y_peer = at(z, 1 - y, x)

    def next_x(d):
        return lax.rem(x + d, NX)

    def next_z(d):
        return lax.rem(z + d, NZ)

    def next_lab(d):
        return lax.rem(j + d, NLAB)

    def across(d):
        return {**y_peer, "lab": next_lab(d)}

    def rows(index, size):
        return pl.ds(pl.multiple_of(index * size, size), size)

    def push(name, d, src, dst, device):
        return pltpu.make_async_remote_copy(
            src_ref=src,
            dst_ref=dst,
            send_sem=getattr(s, "send_" + name).at[d],
            recv_sem=getattr(s, "recv_" + name).at[d],
            device_id=device,
            device_id_type=MESH,
        )

    sent = []

    def start(count, copies):
        each(count, lambda d: copies(d).start())
        sent.append((count, copies))

    def arrive(count, copies):
        each(count, lambda d: copies(d).wait_recv())

    loads = [
        pltpu.make_async_copy(source, target, s.load.at[k])
        for k, (source, target) in enumerate(
            (
                (qh, s.qh),
                (ids, s.ids_raw),
                (used, s.used),
                (qp.at[:, pl.ds(0, cut)], s.wx.at[y, x]),
                (qp.at[:, pl.ds(cut, width - cut)], s.wz.at[z, y]),
                (lp, s.lp.at[y, x]),
                (lh, s.lh),
            )
        )
    ]
    for load in loads:
        load.start()

    barrier = pltpu.get_barrier_semaphore()

    def greet(device):
        pl.semaphore_signal(barrier, inc=1, device_id=device, device_id_type=MESH)

    each(NX, lambda d: greet(at(z, y, next_x(d))))
    each(NZ, lambda d: greet(at(next_z(d), y, x)))
    greet(y_peer)
    each(NX, lambda d: greet(at(z, 1 - y, next_x(d))))
    each(NZ, lambda d: greet(at(next_z(d), 1 - y, x)))
    each(NLAB, lambda d: greet({"lab": next_lab(d)}))
    each(NLAB, lambda d: greet(across(d)))

    loads[0].wait()
    for k in range(NX):
        s.q1_send[k] = jnp.concatenate(
            [s.qh[:, (NX * r + k) * e_row : (NX * r + k + 1) * e_row] for r in range(NZ * NY)], axis=1
        )
    for k in range(NZ * NY):
        s.qx_send[k] = s.qh[:, k * e_b : (k + 1) * e_b]
    for nx in range(NX):
        for ny in range(NY):
            first = [(NX * (NY * r + ny) + nx) * e_row for r in range(NZ)]
            s.qz_send[NY * nx + ny] = jnp.concatenate([s.qh[:, f : f + e_row] for f in first], axis=1)
    loads[1].wait()
    loads[2].wait()
    slots = ids.shape[0]
    s.ids_send[...] = jnp.full(s.ids_send.shape, -1, jnp.int32)
    slot_at = lax.broadcasted_iota(jnp.int32, ids.shape, 0)
    s.ids_send[:, :own] = jnp.where(slot_at < s.used[...], s.ids_raw[...], -1)
    pl.semaphore_wait(barrier, 2 * (NX - 1) + 2 * (NZ - 1) + 1 + 2 * (NLAB - 1))

    x_cols, z_cols = pl.ds(0, cut), pl.ds(cut, width - cut)

    def w_yx(d):
        return push("w_yx", d, qp.at[:, x_cols], s.wx.at[y, x], y_peer)

    def w_yz(d):
        return push("w_yz", d, qp.at[:, z_cols], s.wz.at[z, y], y_peer)

    def w_x(d):
        return push("w_x", d, qp.at[:, x_cols], s.wx.at[y, x], at(z, y, next_x(d)))

    def w_z(d):
        return push("w_z", d, qp.at[:, z_cols], s.wz.at[z, y], at(next_z(d), y, x))

    def w_fx(d):
        return push("w_fx", d, s.wx.at[1 - y, x], s.wx.at[1 - y, x], at(z, y, next_x(d)))

    def w_fz(d):
        return push("w_fz", d, s.wz.at[z, 1 - y], s.wz.at[z, 1 - y], at(next_z(d), y, x))

    def q0(d):
        return push("q0", d, qh.at[:, rows(next_z(d), e_z)], s.q0.at[z], at(next_z(d), y, x))

    def q1(d):
        return push("q1", d, s.q1_send.at[next_x(d)], s.q1.at[x], at(z, y, next_x(d)))

    def l_x(d):
        return push("l_x", d, lp, s.lp.at[y, x], at(z, y, next_x(d)))

    def l_own(d):
        return push("l_own", d, lp, s.lp.at[y, x], y_peer)

    def l_y(d):
        block_at = s.lp.at[y, lax.rem(x + NX - d, NX)]
        return push("l_y", d, block_at, block_at, y_peer)

    start(NX, l_x)
    start(2, w_yx)
    start(2, w_yz)
    start(2, l_own)
    start(NX, w_x)
    start(NZ, w_z)
    start(NZ, q0)
    start(NX, q1)

    def i_y(d):
        return push("i_y", d, s.ids_send, s.ids.at[x, y], y_peer)

    def i_x(d):
        return push("i_x", d, s.ids.at[x], s.ids.at[x], at(z, y, next_x(d)))

    def i_z(d):
        return push("i_z", d, s.ids, s.ids, at(next_z(d), y, x))

    holder = z == j

    @pl.when(holder)
    def _():
        i_y(1).start()
        s.ids[x, y] = s.ids_send[...]
        i_y(1).wait_recv()
        each(NX, lambda d: i_x(d).start())

    s.q0[z] = s.qh[:, rows(z, e_z)]
    s.q1[x] = s.q1_send[x]
    arrive(2, w_yx)
    start(NX, w_fx)
    arrive(2, w_yz)
    start(NZ, w_fz)

    @pl.when(holder)
    def _():
        arrive(NX, i_x)
        each(NZ, lambda d: i_z(d).start())

    def ids_arrive():
        @pl.when(jnp.logical_not(holder))
        def _():
            i_z(lax.rem(z - j + NZ, NZ)).wait_recv()

    def ids_sent():
        @pl.when(holder)
        def _():
            i_y(1).wait_send()
            each(NX, lambda d: i_x(d).wait_send())
            each(NZ, lambda d: i_z(d).wait_send())

    arrive(NX, l_x)
    start(NX, l_y)

    arrive(NZ, q0)
    arrive(NX, w_x)
    loads[3].wait()
    arrive(NX, w_fx)
    s.part_z[...] = dot(s.q0[...].reshape(block, e_z), s.wx[...].reshape(e_z, cut)).reshape(NZ, own, cut)

    def b_z(d):
        return push("b_z", d, s.part_z.at[next_z(d)], s.sum_z.at[z], at(next_z(d), y, x))

    start(NZ, b_z)
    arrive(NX, q1)
    arrive(NZ, w_z)
    loads[4].wait()
    arrive(NZ, w_fz)
    s.part_x[...] = dot(s.q1[...].reshape(block, e_z), s.wz[...].reshape(e_z, width - cut)).reshape(NX, own, width - cut)

    def b_x(d):
        return push("b_x", d, s.part_x.at[next_x(d)], s.sum_x.at[x], at(z, y, next_x(d)))

    start(NX, b_x)
    s.sum_z[z] = s.part_z[z]
    s.sum_x[x] = s.part_x[x]

    ids_arrive()
    local = s.ids[...].reshape(NX * NY * slots, s.ids.shape[3]).T - n_label * me
    wide = 256
    for c in range(n_label // wide):
        column = lax.broadcasted_iota(jnp.int32, (own, wide), 1) + c * wide
        tally = jnp.zeros((8, wide), F32)
        for k in range(NX * NY):
            found = jnp.zeros((own, wide), F32)
            for slot in range(k * slots, (k + 1) * slots):
                found += jnp.where(local[:own, slot : slot + 1] == column, 1.0, 0.0)
            s.mask[k * own : (k + 1) * own, c * wide : (c + 1) * wide] = found
            tally += jnp.sum(found.reshape(own // 8, 8, wide), axis=0)
        s.c_part[:, c * wide : (c + 1) * wide] = tally

    def count(d):
        return push("count", d, s.c_part, s.c_recv.at[j], {"lab": next_lab(d)})

    start(NLAB, count)
    s.c_recv[j] = s.c_part[...]

    arrive(NZ, b_z)
    s.qe[z, :, :cut] = (s.sum_z[0] + s.sum_z[1] + s.sum_z[2] + s.sum_z[3]).astype(BF16)
    arrive(NX, b_x)
    s.qe[z, :, cut:] = (s.sum_x[0] + s.sum_x[1] + s.sum_x[2] + s.sum_x[3]).astype(BF16)

    def q_all(d):
        return push("q_all", d, s.qe.at[z], s.qe.at[z], at(next_z(d), y, x))

    start(NZ, q_all)
    loads[5].wait()
    arrive(2, l_own)
    arrive(NX, l_y)
    arrive(NZ, q_all)

    part = dot(s.qe[...].reshape(block, width), s.lp[...].reshape(d_z, width), COLS)
    s.t_part[...] = part.astype(BF16).reshape(NLAB, own, d_z)

    def t_sum(d):
        return push("t_sum", d, s.t_part.at[next_lab(d)], s.t_recv.at[y, j], {"lab": next_lab(d)})

    def t_cross(d):
        return push("t_cross", d, s.t_part.at[next_lab(d)], s.t_recv.at[y, j], across(d))

    start(NLAB, t_sum)
    start(NLAB + 1, t_cross)
    s.t_recv[y, j] = s.t_part[j]

    arrive(NLAB, t_sum)
    arrive(NLAB + 1, t_cross)
    mine = rows(z, d_z)
    total = s.t_recv[:, 0].astype(F32)
    for k in range(1, NLAB):
        total += s.t_recv[:, k].astype(F32)
    s.t[x, :, :, mine] = total.astype(BF16)

    def t_x(d):
        return push("t_x", d, s.t.at[x, 0, :, mine], s.t.at[x, 0, :, mine], at(z, y, next_x(d)))

    def t_z(d):
        return push("t_z", d, s.t.at[x, 1, :, mine], s.t.at[x, 1, :, mine], at(next_z(d), y, x))

    def t_xz(k):
        tile = s.t.at[lax.rem(x + NX - k, NX), 0, :, mine]
        return lambda d: push("t_xz", NZ * k + d, tile, tile, at(next_z(d), y, x))

    def t_zx(k):
        tile = s.t.at[x, 1, :, rows(lax.rem(z + NZ - k, NZ), d_z)]
        return lambda d: push("t_zx", NX * k + d, tile, tile, at(z, y, next_x(d)))

    def q_y(d):
        return push("q_y", d, s.qe, s.qe_peer, y_peer)

    start(NX, t_x)
    start(NZ, t_z)
    start(NZ, t_xz(0))
    start(NX, t_zx(0))
    for k in range(1, NX):
        t_x(k).wait_recv()
        start(NZ, t_xz(k))
        t_z(k).wait_recv()
        start(NX, t_zx(k))
    arrive(NLAB, count)
    counts = jnp.sum(s.c_recv[0] + s.c_recv[1] + s.c_recv[2] + s.c_recv[3], axis=0, keepdims=True)
    s.weight[...] = (1.0 - 0.99) / (1.0 - jnp.exp((counts + 1.0) * float(np.log(np.float64(np.float32(0.99))))))

    loads[6].wait()
    for k in range(NX):
        arrive(NZ, t_xz(k))
        arrive(NX, t_zx(k))

    def in_b(d):
        return lax.rem(z + lax.div(d, NY), NZ), lax.rem(y + lax.rem(d, NY), NY)

    def in_c(d):
        return lax.rem(x + lax.div(d, NY), NX), lax.rem(y + lax.rem(d, NY), NY)

    spot_b, spot_c = NY * z + y, NY * x + y

    def q_bx(d):
        nz, ny = in_b(d)
        return push("q_bx", d, s.qx_send.at[NY * nz + ny], s.qx.at[spot_b], at(nz, ny, x))

    def q_bz(d):
        nx, ny = in_c(d)
        return push("q_bz", d, s.qz_send.at[NY * nx + ny], s.qz.at[spot_c], at(z, ny, nx))

    start(NZ * NY, q_bx)
    start(NX * NY, q_bz)
    s.qx[spot_b] = s.qx_send[spot_b]
    s.qz[spot_c] = s.qz_send[spot_c]

    start(2, q_y)
    tall = 32

    def label_block(c, carry):
        cols = rows(c, wide)
        s.logit[...] = dot(s.t[...].reshape(here, wide_d), s.lh[cols, :], COLS) * temper
        weight = s.weight[:, cols]

        def row_block(r, loss):
            some = rows(r, tall)
            value = s.logit[some, :]
            hit = s.mask[some, cols] > 0.0
            value = jnp.where(hit, -value, value)
            small = jnp.exp(-jnp.abs(value))
            soft = jnp.maximum(value, 0.0) + jnp.log1p(small)
            over = 1.0 / (1.0 + small)
            under = small * over
            high = value >= 0.0
            chance, rest = jnp.where(high, over, under), jnp.where(high, under, over)
            square = chance * chance
            slope = weight * (square * (chance + 2.0 * rest * soft)) * temper
            s.gl[some, cols] = jnp.where(hit, -slope, slope).astype(BF16)
            return loss + jnp.sum((weight * (square * soft)).reshape(tall // 8, 8, wide), axis=0)

        s.l_part[:, cols] = lax.fori_loop(0, here // tall, row_block, jnp.zeros((8, wide), F32), unroll=True)
        return carry

    lax.fori_loop(0, n_label // wide, label_block, 0)

    def u_z(d):
        return push("u_z", d, s.u_part.at[:, 0, :, rows(next_z(d), d_z)], s.u_rz.at[z], at(next_z(d), y, x))

    def u_x(d):
        return push("u_x", d, s.u_part.at[next_x(d), 1], s.u_rx.at[x], at(z, y, next_x(d)))

    def u_zx(d):
        return push("u_zx", d, s.u_sz.at[next_x(d)], s.u_rzx.at[x], at(z, y, next_x(d)))

    def u_xz(d):
        return push("u_xz", d, s.u_sx.at[:, rows(next_z(d), d_z)], s.u_rxz.at[z], at(next_z(d), y, x))

    def u_block(d):
        cols = rows(next_z(d), d_z)
        part = dot(s.gl[...], s.lh[:, cols])
        s.u_part[:, :, :, cols] = part.astype(BF16).reshape(NX, NY, own, d_z)

    def u_turn(d):
        u_block(d)
        u_z(d).start()

    each(NZ, u_turn)
    sent.append((NZ, u_z))
    u_block(0)
    start(NX, u_x)

    def loss_sum(d):
        return push("loss", d, s.l_part, s.l_recv.at[j], {"lab": next_lab(d)})

    start(NLAB, loss_sum)
    s.l_recv[j] = s.l_part[...]
    arrive(NZ, u_z)
    half = s.u_part[:, 0, :, mine].astype(F32)
    for d in range(1, NZ):
        half += s.u_rz[next_z(d)].astype(F32)
    s.u_sz[...] = half.astype(BF16)
    start(NX, u_zx)
    arrive(NX, u_x)
    half = s.u_part[x, 1].astype(F32)
    for d in range(1, NX):
        half += s.u_rx[next_x(d)].astype(F32)
    s.u_sx[...] = half.astype(BF16)
    start(NZ, u_xz)
    arrive(NX, u_zx)
    half = s.u_sz[x].astype(F32)
    for d in range(1, NX):
        half += s.u_rzx[next_x(d)].astype(F32)
    s.back[0] = half
    arrive(NZ, u_xz)
    half = s.u_sx[:, mine].astype(F32)
    for d in range(1, NZ):
        half += s.u_rxz[next_z(d)].astype(F32)
    s.back[1] = half

    s.u_send[...] = s.back[...].astype(BF16)

    def u_all(d):
        return push("u_all", d, s.u_send.at[y], s.u.at[y, j], {"lab": next_lab(d)})

    def u_cross(d):
        return push("u_cross", d, s.u_send.at[1 - y], s.u.at[y, j], across(d))

    start(NLAB, u_all)
    start(NLAB + 1, u_cross)
    s.u[y, j] = s.u_send[y]
    arrive(NLAB, u_all)
    arrive(NLAB + 1, u_cross)
    u = [s.u[k].reshape(block, d_z) for k in range(NY)]

    s.u_sum[...] = (u[0].astype(F32) + u[1].astype(F32)).astype(BF16)

    def u_y(d):
        return push("u_y", d, s.u_sum, s.u_peer, y_peer)

    start(2, u_y)
    l_proj = s.lp[...].reshape(d_z, width)
    part = (dot(u[0], l_proj) + dot(u[1], l_proj)).reshape(NZ, own, width)
    s.g_part[...] = part
    s.g_send[...] = part.astype(BF16)

    def g_sum(d):
        return push("g_sum", d, s.g_send.at[next_z(d)], s.g_recv.at[z], at(next_z(d), y, x))

    start(NZ, g_sum)

    qe = s.qe[...].reshape(block, width)
    part = dot(u[0], qe, ROWS) + dot(u[1], qe, ROWS)
    arrive(2, q_y)
    arrive(2, u_y)
    part += dot(s.u_peer[...], s.qe_peer[...].reshape(block, width), ROWS)
    s.k_both[...] = part.reshape(NY, NX, d_row, width)
    s.k_send[...] = s.k_both[y].astype(BF16)

    def k_x(d):
        return push("k_x", d, s.k_send.at[next_x(d)], s.k_recv.at[x], at(z, y, next_x(d)))

    start(NX, k_x)
    arrive(NZ, g_sum)
    total = s.g_part[z]
    for d in range(1, NZ):
        total += s.g_recv[next_z(d)].astype(F32)
    gqe_out[...] = total
    s.ge[...] = total.astype(BF16)

    def g_yx(d):
        return push("g_yx", d, s.ge.at[:, x_cols], s.gx.at[spot_b], y_peer)

    def g_yz(d):
        return push("g_yz", d, s.ge.at[:, z_cols], s.gz.at[spot_c], y_peer)

    def g_z(d):
        return push("g_z", d, s.ge.at[:, x_cols], s.gx.at[spot_b], at(next_z(d), y, x))

    def g_x(d):
        return push("g_x", d, s.ge.at[:, z_cols], s.gz.at[spot_c], at(z, y, next_x(d)))

    def g_fz(d):
        other = s.gx.at[NY * z + 1 - y]
        return push("g_fz", d, other, other, at(next_z(d), y, x))

    def g_fx(d):
        other = s.gz.at[NY * x + 1 - y]
        return push("g_fx", d, other, other, at(z, y, next_x(d)))

    start(2, g_yx)
    start(2, g_yz)
    start(NZ, g_z)
    start(NX, g_x)
    arrive(2, g_yx)
    start(NZ, g_fz)
    arrive(2, g_yz)
    start(NX, g_fx)
    s.gx[spot_b] = s.ge[:, :cut]
    s.gz[spot_c] = s.ge[:, cut:]
    arrive(NLAB, loss_sum)
    losses = jnp.sum(s.l_recv[0] + s.l_recv[1] + s.l_recv[2] + s.l_recv[3], axis=0, keepdims=True)
    loss_out[...] = losses / (NQRY * own)
    arrive(NZ * NY, q_bx)
    arrive(NX * NY, q_bz)

    arrive(NZ, g_z)
    arrive(NZ, g_fz)
    part = dot(s.qx[...].reshape(here, e_b), s.gx[...].reshape(here, cut), ROWS).reshape(NX, e_row, cut)
    s.px_part[...] = part
    s.px_send[...] = part.astype(BF16)

    def p_x(d):
        return push("p_x", d, s.px_send.at[next_x(d)], s.px_recv.at[x], at(z, y, next_x(d)))

    start(NX, p_x)
    arrive(NX, g_x)
    arrive(NX, g_fx)
    part = dot(s.qz[...].reshape(here, e_b), s.gz[...].reshape(here, width - cut), ROWS).reshape(NZ, e_row, width - cut)
    s.pz_part[...] = part
    s.pz_send[...] = part.astype(BF16)

    def p_z(d):
        return push("p_z", d, s.pz_send.at[next_z(d)], s.pz_recv.at[z], at(next_z(d), y, x))

    start(NZ, p_z)

    arrive(NX, k_x)
    total = s.k_both[y, x]
    for d in range(1, NX):
        total += s.k_recv[next_x(d)].astype(F32)
    glp_out[...] = total
    arrive(NX, p_x)
    total = s.px_part[x]
    for d in range(1, NX):
        total += s.px_recv[next_x(d)].astype(F32)
    gqp_out[:, :cut] = total
    arrive(NZ, p_z)
    total = s.pz_part[z]
    for d in range(1, NZ):
        total += s.pz_recv[next_z(d)].astype(F32)
    gqp_out[:, cut:] = total

    for number, copies in sent:
        each(number, lambda d: copies(d).wait_send())
    ids_sent()


class Scratch:
    def __init__(self, names, refs):
        for name, ref in zip(names, refs):
            setattr(self, name, ref)


def shards(query_hidden, query_proj, label_hidden, label_proj, pos_ids, pos_count):
    own, wide_e = query_hidden.shape
    n_label, wide_d = label_hidden.shape
    e_row, width = query_proj.shape
    d_row = label_proj.shape[0]
    slots = pos_ids.shape[1]
    e_z, d_z, e_b = NX * NY * e_row, NX * NY * d_row, NX * e_row
    here, block = NX * NY * own, NZ * own
    cut = width // 256 * 128
    rest = width - cut
    scratch = {
        "qh": ((own, wide_e), BF16),
        "ids_raw": ((slots, own), jnp.int32),
        "used": ((1, own), jnp.int32),
        "ids_send": ((slots, 128), jnp.int32),
        "ids": ((NX, NY, slots, 128), jnp.int32),
        "lh": ((n_label, wide_d), BF16),
        "lp": ((NY, NX, d_row, width), BF16),
        "wx": ((NY, NX, e_row, cut), BF16),
        "wz": ((NZ, NY, e_row, rest), BF16),
        "q0": ((NZ, own, e_z), BF16),
        "q1_send": ((NX, own, e_z), BF16),
        "q1": ((NX, own, e_z), BF16),
        "qx_send": ((NZ * NY, own, e_b), BF16),
        "qx": ((NZ * NY, own, e_b), BF16),
        "qz_send": ((NX * NY, own, e_b), BF16),
        "qz": ((NX * NY, own, e_b), BF16),
        "part_z": ((NZ, own, cut), F32),
        "sum_z": ((NZ, own, cut), F32),
        "part_x": ((NX, own, rest), F32),
        "sum_x": ((NX, own, rest), F32),
        "mask": ((here, n_label), F32),
        "c_part": ((8, n_label), F32),
        "c_recv": ((NLAB, 8, n_label), F32),
        "weight": ((1, n_label), F32),
        "qe": ((NZ, own, width), BF16),
        "t_part": ((NLAB, own, d_z), BF16),
        "t_recv": ((NY, NLAB, own, d_z), BF16),
        "t": ((NX, NY, own, wide_d), BF16),
        "logit": ((here, 256), F32),
        "gl": ((here, n_label), BF16),
        "l_part": ((8, n_label), F32),
        "l_recv": ((NLAB, 8, n_label), F32),
        "u_part": ((NX, NY, own, wide_d), BF16),
        "u_rz": ((NZ, NX, own, d_z), BF16),
        "u_rx": ((NX, own, wide_d), BF16),
        "u_sz": ((NX, own, d_z), BF16),
        "u_sx": ((own, wide_d), BF16),
        "u_rzx": ((NX, own, d_z), BF16),
        "u_rxz": ((NZ, own, d_z), BF16),
        "back": ((NY, own, d_z), F32),
        "u_send": ((NY, own, d_z), BF16),
        "u": ((NY, NLAB, own, d_z), BF16),
        "u_sum": ((block, d_z), BF16),
        "u_peer": ((block, d_z), BF16),
        "qe_peer": ((NZ, own, width), BF16),
        "g_part": ((NZ, own, width), F32),
        "g_send": ((NZ, own, width), BF16),
        "g_recv": ((NZ, own, width), BF16),
        "ge": ((own, width), BF16),
        "gx": ((NZ * NY, own, cut), BF16),
        "gz": ((NX * NY, own, rest), BF16),
        "k_both": ((NY, NX, d_row, width), F32),
        "k_send": ((NX, d_row, width), BF16),
        "k_recv": ((NX, d_row, width), BF16),
        "px_part": ((NX, e_row, cut), F32),
        "px_send": ((NX, e_row, cut), BF16),
        "px_recv": ((NX, e_row, cut), BF16),
        "pz_part": ((NZ, e_row, rest), F32),
        "pz_send": ((NZ, e_row, rest), BF16),
        "pz_recv": ((NZ, e_row, rest), BF16),
    }
    scratch = {name: pltpu.VMEM(*spec) for name, spec in scratch.items()}
    scratch["load"] = pltpu.SemaphoreType.DMA((7,))
    pairs = ("w_yx", "w_yz", "l_own", "i_y", "g_yx", "g_yz", "q_y", "u_y")
    fours = (
        "w_x", "w_z", "w_fx", "w_fz", "q0", "q1", "l_x", "l_y", "i_x", "i_z", "b_z", "b_x", "count", "q_all", "t_sum",
        "t_x", "t_z", "u_z", "u_x", "u_zx", "u_xz", "loss", "u_all", "g_sum", "g_z", "g_x", "g_fz", "g_fx", "k_x", "p_x", "p_z",
    )
    fives, eights = ("t_cross", "u_cross"), ("q_bx", "q_bz")
    sixteens = ("t_xz", "t_zx")
    for number, group in ((2, pairs), (4, fours), (5, fives), (8, eights), (16, sixteens)):
        for name in group:
            scratch["send_" + name] = pltpu.SemaphoreType.DMA((number,))
            scratch["recv_" + name] = pltpu.SemaphoreType.DMA((number,))
    names = tuple(scratch)

    def kernel(*refs):
        step_kernel(wide_e ** (-0.5), cut, *refs[:10], Scratch(names, refs[10:]))

    arrays = [
        pltpu.with_memory_space_constraint(a, pltpu.HBM)
        for a in (query_hidden, query_proj, label_hidden, label_proj, pos_ids.T, pos_count.reshape(1, own))
    ]
    gqp, glp, loss, gqe = pl.pallas_call(
        kernel,
        out_shape=(
            jax.ShapeDtypeStruct((e_row, width), F32),
            jax.ShapeDtypeStruct((d_row, width), F32),
            jax.ShapeDtypeStruct((1, n_label), F32),
            jax.ShapeDtypeStruct((own, width), F32),
        ),
        in_specs=[pl.BlockSpec(memory_space=pltpu.HBM)] * 6,
        out_specs=(pl.BlockSpec(memory_space=pltpu.VMEM),) * 4,
        scratch_shapes=list(scratch.values()),
        compiler_params=pltpu.CompilerParams(
            collective_id=0, has_side_effects=True, vmem_limit_bytes=48 << 20
        ),
        name="focal_step",
    )(*arrays)
    return gqp, glp, loss.reshape(n_label), gqe


def solution(mesh):
    in_specs = (
        P("qry", None),
        P("qry", "lab"),
        P("qry", None),
        P("qry", "lab"),
        P("qry", None),
        P("qry"),
    )
    out_specs = (P("qry", "lab"), P("qry", "lab"), P("qry"), P("qry", "lab"))
    return jax.shard_map(shards, mesh=mesh, in_specs=in_specs, out_specs=out_specs, check_vma=False)
```
